512 devices in a mesh: dp: 128 (over y, z, core), mp: 4 (over x).
Axes of the slice: x: 4, y: 8, z: 8, core: 2. Of those that a mesh axis runs over, the one named last changes fastest.
Arguments:
- grad_cot: bfloat16 [131072, 2048], P('dp', 'mp'), may hold values from -0.1875 to 0.1875
- grad_hidden: bfloat16 [131072, 1024], P('dp'), may hold values from -6 to 6
- old_place: int32 [128], replicated, may hold values from 0 to 31
- master: float32 [32, 4, 524288], P(None, 'mp', 'dp'), may hold values from -0.125 to 0.125
- moment_one: float32 [32, 4, 524288], P(None, 'mp', 'dp'), may hold values from -2 to 2
- moment_two: float32 [32, 4, 524288], P(None, 'mp', 'dp'), may hold values from 0.05 to 1
- new_place: int32 [128], replicated, may hold values from 0 to 31
- rows: bfloat16 [16384, 2048], P('dp', 'mp'), may hold values from -6 to 6
- dest: int32 [16384], P('dp'), may hold values from 0 to 127, as said below
- counts: int32 [128], P('dp'), may hold values from 112 to 128, as said below
Outputs:
- master_new: float32 [32, 4, 524288], P(None, 'mp', 'dp')
- moment_one_new: float32 [32, 4, 524288], P(None, 'mp', 'dp')
- moment_two_new: float32 [32, 4, 524288], P(None, 'mp', 'dp')
- projected: bfloat16 [16384, 1024], P('dp', 'mp')
The draws below stay inside these ranges and needn't reach their ends.
Inputs may be any that keep to these rules, and one draw needn't show every extreme that they name: `dest`: each token shard's 128 rows name exactly 64 distinct replica groups, 2 rows each, so no replica group receives more than 2 rows from one shard; in every draw one replica group is named by 2 rows of every shard. `counts`: some shard is full and some shard has the fewest live rows allowed.
All inputs are finite; a program needn't handle non-finite values.
Results may differ from the reference program's by a relative error of at most 0.005.
Values may be sent and summed in bfloat16 or wider, within the bound.
A program may use at most 64 MiB of HBM per device.

```python
import math
import jax
import jax.numpy as jnp
from jax import lax

D = 2048
FF = 1024
EXPERTS = 32
REPLICA_ROWS = 1024
ROWS_DEV = 128
TOKENS = 16384
REPLICA_TOKENS = 131072
GROUPS = 64
CAP = 2
SLAB = 524288
N_DP = 128
N_MP = 4


def draw_dest(key, part):
    shards = TOKENS // ROWS_DEV
    key_order, key_offset, key_rows = jax.random.split(jax.random.fold_in(key, 101), 3)
    ranking = jax.random.permutation(key_order, shards)
    offsets = jax.random.randint(key_offset, (shards, 1), 0, shards - 1)
    groups = jnp.arange(GROUPS)[None, :]
    spread = 1 + (offsets + groups - 1) % (shards - 1)
    chosen = jnp.where(groups == 0, 0, spread)
    group_dest = ranking[chosen]
    row_keys = jax.random.split(key_rows, shards)
    positions = jax.vmap(lambda one_key: jax.random.permutation(one_key, ROWS_DEV))(row_keys)
    labels = positions // CAP
    picked = jnp.take_along_axis(group_dest, labels, axis=1)
    return picked.reshape(TOKENS).astype(jnp.int32)


def draw_counts(key, part):
    shards = TOKENS // ROWS_DEV
    lowest = ROWS_DEV - ROWS_DEV // 8
    key_level, key_extremes = jax.random.split(jax.random.fold_in(key, 202))
    levels = jax.random.randint(key_level, (shards,), lowest, ROWS_DEV + 1)
    extremes = jax.random.permutation(key_extremes, shards)
    levels = levels.at[extremes[0]].set(ROWS_DEV).at[extremes[1]].set(lowest)
    return levels.astype(jnp.int32)


def place_ends(entries, stream_key, low, top_value):
    spot = [jax.random.randint(jax.random.fold_in(stream_key, axis), (), 0, length) for axis, length in enumerate(entries.shape)]
    longest = entries.shape.index(max(entries.shape))
    neighbour = spot[:longest] + [(spot[longest] + 1) % entries.shape[longest]] + spot[longest + 1:]
    return entries.at[tuple(spot)].set(low).at[tuple(neighbour)].set(top_value)


def block_scale(key, extent, cuts, smallest, top_value):
    def one(dim, blocks):
        heights = jax.random.uniform(jax.random.fold_in(jax.random.fold_in(key, 6), dim), (blocks,), jnp.float32, smallest / len(cuts), top_value / len(cuts))
        return jnp.repeat(jnp.exp(heights), extent[dim] // blocks).reshape((-1,) + (1,) * (len(extent) - dim - 1))

    loudness = one(*cuts[0])
    for cut in cuts[1:]:
        loudness = loudness * one(*cut)
    return loudness


def centred(key, shape, width, bound, cuts=(), held_as=jnp.bfloat16):
    values = width * jax.random.normal(key, shape, jnp.float32)
    if cuts:
        values = values * block_scale(key, shape, cuts, -0.22, 0.18)
    return jnp.clip(values, -bound, bound).astype(held_as)


def setup_inputs(seed: int = 0) -> dict:
    key_of = jax.random.split(jax.random.key(seed), 11)
    grad_cot = centred(key_of[0], (REPLICA_TOKENS, D), REPLICA_ROWS ** -0.5, 0.1875, ((0, 128), (1, 4)))
    grad_hidden = centred(key_of[1], (REPLICA_TOKENS, FF), 1.0, 6.0, ((0, 128),))
    old_place = place_ends(jax.random.randint(key_of[2], (N_DP,), 0, EXPERTS), jax.random.fold_in(key_of[2], 1), 0, EXPERTS - 1).astype(jnp.int32)
    master = centred(key_of[3], (EXPERTS, N_MP, SLAB), D ** -0.5, 0.125, ((1, 4), (2, 128)), jnp.float32)
    moment_one = centred(key_of[4], (EXPERTS, N_MP, SLAB), 0.3, 2.0, ((1, 4), (2, 128)), jnp.float32)
    moment_two = jnp.clip(jnp.exp(math.log(1.0) - 2.9957323 * jax.random.uniform(key_of[5], (EXPERTS, N_MP, SLAB), jnp.float32) ** block_scale(key_of[5], (EXPERTS, N_MP, SLAB), ((1, 4), (2, 128)), -0.2, 0.2)), 0.05, 1.0)
    new_place = place_ends(jax.random.randint(key_of[6], (N_DP,), 0, EXPERTS), jax.random.fold_in(key_of[6], 1), 0, EXPERTS - 1).astype(jnp.int32)
    rows = centred(key_of[7], (TOKENS, D), 1.0, 6.0, ((0, 128), (1, 4)))
    dest = draw_dest(jax.random.fold_in(key_of[10], 71), 0)
    counts = draw_counts(jax.random.fold_in(key_of[10], 71), 0)
    return dict(grad_cot=grad_cot, grad_hidden=grad_hidden, old_place=old_place, master=master, moment_one=moment_one, moment_two=moment_two, new_place=new_place, rows=rows, dest=dest, counts=counts)


beta_first = 0.9
beta_second = 0.95
learn_rate = 0.01
decay_rate = 0.1
adam_eps = 1e-08
bias_first = 1.0 - 0.9 ** 10
bias_second = 1.0 - 0.95 ** 10

def adam_update(gradient, master, moment_one, moment_two):
    first_new = beta_first * moment_one + (1.0 - beta_first) * gradient
    second_new = beta_second * moment_two + (1.0 - beta_second) * gradient * gradient
    step_dir = first_new / bias_first / (jnp.sqrt(second_new / bias_second) + adam_eps)
    updated = master - learn_rate * (step_dir + decay_rate * master)
    return (updated, first_new, second_new)

def reference(grad_cot, grad_hidden, old_place, master, moment_one, moment_two, new_place, rows, dest, counts):
    experts = master.shape[0]

    def add_replica(running, replica):
        cot_block = lax.dynamic_slice_in_dim(grad_cot, replica * REPLICA_ROWS, REPLICA_ROWS, 0).astype(jnp.float32)
        hid_block = lax.dynamic_slice_in_dim(grad_hidden, replica * REPLICA_ROWS, REPLICA_ROWS, 0).astype(jnp.float32)
        partial_value = jnp.dot(cot_block.T, hid_block, precision=lax.Precision.HIGHEST, preferred_element_type=jnp.float32)
        expert = old_place[replica]
        current = lax.dynamic_index_in_dim(running, expert, 0, keepdims=False)
        return (lax.dynamic_update_index_in_dim(running, current + partial_value, expert, 0), None)
    running, unused = lax.scan(add_replica, jnp.zeros((experts, D, FF), jnp.float32), jnp.arange(N_DP, dtype=jnp.int32))
    gradient = running.reshape(experts, N_MP, D * FF // N_MP)
    updated, first_new, second_new = adam_update(gradient, master, moment_one, moment_two)
    weights = updated.astype(jnp.bfloat16).reshape(experts, D, FF)
    token_ids = jnp.arange(TOKENS, dtype=jnp.int32)
    row_live = token_ids % ROWS_DEV < counts[token_ids // ROWS_DEV]
    masked = jnp.where(row_live[:, None], rows, jnp.zeros((), jnp.bfloat16))
    sorted_ids = jnp.argsort(dest, stable=True).astype(jnp.int32)
    replica_loads = lax.optimization_barrier(jnp.sum((dest[None, :] == jnp.arange(N_DP, dtype=jnp.int32)[:, None]).astype(jnp.int32), axis=1))
    starts = (jnp.cumsum(replica_loads) - replica_loads).astype(jnp.int32)
    window = N_DP * CAP
    padded_ids = jnp.concatenate([sorted_ids, jnp.zeros((window,), jnp.int32)])

    def serve_replica(accum, replica):
        picked_ids = lax.dynamic_slice_in_dim(padded_ids, starts[replica], window, 0)
        inside = jnp.arange(window, dtype=jnp.int32) < replica_loads[replica]
        row_block = masked[picked_ids].astype(jnp.float32)
        weight = lax.dynamic_index_in_dim(weights, new_place[replica], 0, keepdims=False).astype(jnp.float32)
        result = jnp.dot(row_block, weight, precision=lax.Precision.HIGHEST, preferred_element_type=jnp.float32)
        result = lax.optimization_barrier(result.astype(jnp.bfloat16)).astype(jnp.float32)
        result = jnp.where(inside[:, None], result, jnp.zeros((), jnp.float32))
        return (accum.at[picked_ids].add(result), None)
    accum, unused = lax.scan(serve_replica, jnp.zeros((TOKENS, FF), jnp.float32), jnp.arange(N_DP, dtype=jnp.int32))
    projected = accum.astype(jnp.bfloat16)
    return (updated, first_new, second_new, projected)
```

```python
import jax
import jax.numpy as jnp
from jax import lax
from jax.experimental import pallas as pl
from jax.experimental.pallas import tpu as pltpu
from jax.sharding import PartitionSpec as P

MESH = pl.DeviceIdType.MESH
BF = jnp.bfloat16
F32 = jnp.float32
I32 = jnp.int32

NY = 8
NU = 16
NX = 4
EXPERTS = 32

beta_first = 0.9
beta_second = 0.95
learn_rate = 0.01
decay_rate = 0.1
adam_eps = 1e-08
bias_first = 1.0 - 0.9**10
bias_second = 1.0 - 0.95**10


def adam_update(gradient, master, moment_one, moment_two):
    first_new = beta_first * moment_one + (1.0 - beta_first) * gradient
    second_new = beta_second * moment_two + (1.0 - beta_second) * gradient * gradient
    step_dir = first_new / bias_first / (jnp.sqrt(second_new / bias_second) + adam_eps)
    updated = master - learn_rate * (step_dir + decay_rate * master)
    return (updated, first_new, second_new)


def mm(a, b):
    return jnp.dot(a, b, preferred_element_type=F32)


def ones_where(cond):
    return jnp.where(cond, 1.0, 0.0).astype(BF)


def iota(shape, dim):
    return lax.broadcasted_iota(I32, shape, dim)


def swap_index(r, inner_bits, outer_bits, low_bits):
    low = r & ((1 << low_bits) - 1)
    outer = (r >> low_bits) & ((1 << outer_bits) - 1)
    inner = r >> (low_bits + outer_bits)
    return (((outer << inner_bits) | inner) << low_bits) | low


def reorder(first_bits, second_bits, low_bits):
    n = 1 << (first_bits + second_bits + low_bits)
    source = swap_index(iota((n, n), 0), second_bits, first_bits, low_bits)
    return ones_where(iota((n, n), 1) == source)


def kernel(
    cot_h, hid_h, old_ref, mas_h, one_h, two_h, new_s, rows_h, dest_ref, counts_s,
    mas_o, one_o, two_o, proj_o,
    cot, hid, rows, mas, one, two, mas_n, one_n, two_n, proj,
    p_a, p_at, p_c, p_ct, p_s, p_st, own_a, own_b, slots, slots_u,
    row1, row1r, row2, row2r, rowx, rowp,
    ga1, ga1r, ga2, ga2r, gb0, gb1, gb1r, gb2, gb2r,
    wa, wb, xa, xb, ya, yb, oa1, ob1, wa1r, wb1r, wa2r, wb2r,
    ta1, tb1, ta1r, tb1r, ta2, tb2, ta2r, tb2r,
    in_sem, out_sem, loc_sem, snd_sem, rcv_sem,
):
    me = lax.axis_index("dp")
    mp = lax.axis_index("mp")
    y = me // NU
    u = lax.rem(me, NU)

    def peer_y(k):
        t = lax.rem(y + k, NY)
        return t, (t * NU + u, mp)

    def peer_u(k):
        t = lax.rem(u + k, NU)
        return t, (y * NU + t, mp)

    def peer_x(k):
        t = lax.rem(mp + k, NX)
        return t, (me, t)

    rings = {"y": (NY, y, peer_y), "u": (NU, u, peer_u), "x": (NX, mp, peer_x)}

    ins = [(cot_h, cot), (hid_h, hid), (rows_h, rows), (mas_h, mas), (one_h, one), (two_h, two)]
    in_copies = [pltpu.make_async_copy(s, d, in_sem.at[i]) for i, (s, d) in enumerate(ins)]
    for i in (2, 0, 1, 3, 4, 5):
        in_copies[i].start()

    barrier = pltpu.get_barrier_semaphore()
    for n, _, peer in rings.values():

        @pl.loop(1, n)
        def _(k):
            pl.semaphore_signal(barrier, inc=1, device_id=peer(k)[1], device_id_type=MESH)

    def stage(i, ring, src, part, dst, place):
        n, mine, peer = rings[ring]

        def start():
            @pl.loop(1, n)
            def _(k):
                t, device = peer(k)
                pltpu.make_async_remote_copy(
                    src_ref=part(src, t), dst_ref=place(dst, mine), send_sem=snd_sem.at[i],
                    recv_sem=rcv_sem.at[i], device_id=device, device_id_type=MESH,
                ).start()

            pltpu.make_async_copy(part(src, mine), place(dst, mine), loc_sem.at[i]).start()

        return start

    def finish(i, ring, src_all, dst_all, src, part, dst, place):
        n, mine, peer = rings[ring]
        pltpu.make_async_copy(part(src, mine), place(dst, mine), loc_sem.at[i]).wait()
        whole = pltpu.make_async_remote_copy(
            src_ref=src_all(src, n - 1), dst_ref=dst_all(dst, n - 1), send_sem=snd_sem.at[i],
            recv_sem=rcv_sem.at[i], device_id=peer(1)[1], device_id_type=MESH,
        )
        whole.wait_recv()
        return whole

    lead = lambda ref, t: ref.at[t]
    lead_n = lambda ref, n: ref.at[pl.ds(0, n)]
    second = lambda ref, t: ref.at[:, t]
    second_n = lambda ref, n: ref.at[:, pl.ds(0, n)]
    whole_ref = lambda ref, t: ref

    def exchange(i, ring, src, dst, part=lead, place=lead):
        src_all = second_n if part is second else lead_n
        dst_all = second_n if place is second else lead_n
        if part is whole_ref:
            src_all = lambda ref, n: dst_all(dst, n)
        start = stage(i, ring, src, part, dst, place)
        wait = lambda: finish(i, ring, src_all, dst_all, src, part, dst, place)
        return start, wait

    rows1 = exchange(0, "y", row1, row1r)
    rows2 = exchange(1, "u", row2, row2r)
    rowsx = exchange(2, "x", row2r, rowx, part=whole_ref)
    grad_a1 = exchange(3, "y", ga1, ga1r)
    grad_a2 = exchange(4, "u", ga2, ga2r)
    grad_b1 = exchange(5, "u", gb1, gb1r)
    grad_b2 = exchange(6, "y", gb2, gb2r)
    cross_a = exchange(7, "x", wa, xa)
    cross_b = exchange(8, "x", wb, xb)
    weight_a1 = exchange(9, "u", oa1, wa1r, part=second)
    weight_a2 = exchange(10, "y", wa1r, wa2r, part=second)
    weight_b1 = exchange(11, "y", ob1, wb1r)
    weight_b2 = exchange(12, "u", wb1r, wb2r, part=second, place=second)
    back_a1 = exchange(13, "u", ta1, ta1r)
    back_a2 = exchange(14, "y", ta2, ta2r)
    back_b1 = exchange(15, "y", tb1, tb1r)
    back_b2 = exchange(16, "u", tb2, tb2r)
    sent = []

    dest = jnp.broadcast_to(dest_ref[...], (128, 128))
    dest_t = dest.astype(F32).T.astype(I32)
    earlier = (dest == dest_t) & (iota((128, 128), 0) < iota((128, 128), 1))
    rank = jnp.sum(jnp.where(earlier, 1, 0), axis=0, keepdims=True)
    dest_row = dest_ref[...]
    live = iota((1, 128), 1) < counts_s[0]
    slot_y = jnp.where(live, dest_row * 2 + rank, -1)
    slot_u = jnp.where(live, (dest_row & 15) * 16 + (dest_row >> 4) * 2 + rank, -1)
    slots[...] = ones_where(iota((256, 128), 0) == jnp.broadcast_to(slot_y, (256, 128)))
    slots_u[...] = ones_where(iota((256, 128), 0) == jnp.broadcast_to(slot_u, (256, 128)))
    in_copies[2].wait()
    row1[...] = mm(slots[...], rows[...]).astype(BF).reshape(NY, 32, 512)

    p_a[...] = reorder(3, 4, 2)

    pl.semaphore_wait(barrier, NY - 1 + NU - 1 + NX - 1)
    rows1[0]()

    in_copies[0].wait()
    in_copies[1].wait()

    @pl.loop(0, NX)
    def _(b):
        at = pl.multiple_of(b * 256, 256)
        to = pl.multiple_of(b * 128, 128)
        part = lax.dot_general(
            cot[...], hid[:, pl.ds(at, 256)], (((0,), (0,)), ((), ())), preferred_element_type=F32
        ).astype(BF)
        ga1[:, :, pl.ds(to, 128)] = part[:, :128].reshape(NY, 64, 128)
        gb0[:, pl.ds(to, 128)] = part[:, 128:]

    grad_a1[0]()
    gb1[...] = mm(p_a[...], gb0[...]).astype(BF).reshape(NU, 32, 512)
    grad_b1[0]()

    p_at[...] = reorder(4, 3, 2)
    p_s[...] = reorder(3, 4, 1)
    p_st[...] = reorder(4, 3, 1)
    p_c[...] = reorder(2, 5, 2)
    p_ct[...] = reorder(5, 2, 2)
    old = jnp.broadcast_to(old_ref[...], (8, 128)).astype(F32).astype(BF)
    spread_b = ones_where(iota((128, 512), 0) == (iota((128, 512), 1) >> 2))
    col = iota((128, 512), 1)
    spread_a = ones_where(iota((128, 512), 0) == (((col >> 2) & 7) * NU + (col >> 5)))
    for spread, own in ((spread_a, own_a), (spread_b, own_b)):
        holder = mm(old, spread)[0:1].astype(I32)
        wanted = holder * 4 + (iota((1, 512), 1) & 3)
        own[...] = ones_where(iota((128, 512), 0) == jnp.broadcast_to(wanted, (128, 512)))

    sent.append(rows1[1]())
    row2[...] = mm(p_s[...], row1r[...].reshape(256, 512)).astype(BF).reshape(NU, 16, 512)

    sent.append(grad_a1[1]())
    ga2[...] = mm(p_a[...], ga1r[...].reshape(512, 512)).astype(BF).reshape(NU, 32, 512)
    grad_a2[0]()
    sent.append(grad_b1[1]())
    gb2[...] = mm(p_at[...], gb1r[...].reshape(512, 512)).astype(BF).reshape(NY, 64, 512)
    grad_b2[0]()
    rows2[0]()

    for i in (3, 4, 5):
        in_copies[i].wait()

    def step(got, own, recv, half, out, cross):
        sent.append(got())
        gradient = mm(own[...], recv[...].reshape(512, 512))
        for b in range(NX):
            at = pl.ds(2 * b + half, 128, stride=8)
            updated, first_new, second_new = adam_update(
                gradient[:, b * 128 : (b + 1) * 128], mas[at, :], one[at, :], two[at, :]
            )
            mas_n[at, :] = updated
            one_n[at, :] = first_new
            two_n[at, :] = second_new
            out[b] = updated.astype(BF)
        cross()

    step(grad_a2[1], own_a, ga2r, 0, wa, cross_a[0])
    step(grad_b2[1], own_b, gb2r, 1, wb, cross_b[0])
    outs = [(mas_n, mas_o), (one_n, one_o), (two_n, two_o)]
    out_copies = [pltpu.make_async_copy(s, d, out_sem.at[i]) for i, (s, d) in enumerate(outs)]
    for c in out_copies:
        c.start()

    def place_weights(got, x, table, out, start):
        sent.append(got())
        table[...] = mm(p_c[...], x[...].reshape(512, 128)).astype(BF).reshape(EXPERTS, 16, 128)

        @pl.loop(0, NY)
        def _(a):
            for b in range(NU):
                out[a, b] = table[new_s[a * NU + b]]

        start()

    place_weights(cross_a[1], xa, ya, oa1, weight_a1[0])
    place_weights(cross_b[1], xb, yb, ob1, weight_b1[0])

    sent.append(rows2[1]())
    rowsx[0]()
    sent.append(weight_a1[1]())
    weight_a2[0]()
    sent.append(weight_b1[1]())
    weight_b2[0]()
    sent.append(rowsx[1]())
    for b in range(4):
        lanes = jnp.concatenate(
            [rowx[m, :, :, b * 128 : (b + 1) * 128].reshape(256, 128) for m in range(NX)], axis=1
        )
        rowp[:, b * 512 : (b + 1) * 512] = mm(lanes, p_ct[...]).astype(BF)

    sent.append(weight_a2[1]())
    out_a = mm(rowp[...], wa2r[...].reshape(2048, 128)).astype(BF)
    ta1[...] = out_a.reshape(NU, 16, 128)
    back_a1[0]()
    sent.append(weight_b2[1]())
    out_b = mm(rowp[...], wb2r[...].reshape(2048, 128)).astype(BF)
    tb1[...] = mm(p_st[...], out_b).astype(BF).reshape(NY, 32, 128)
    back_b1[0]()
    sent.append(back_a1[1]())
    ta2[...] = mm(p_st[...], ta1r[...].reshape(256, 128)).astype(BF).reshape(NY, 32, 128)
    back_a2[0]()
    sent.append(back_b1[1]())
    tb2[...] = mm(p_s[...], tb1r[...].reshape(256, 128)).astype(BF).reshape(NU, 16, 128)
    back_b2[0]()

    def pick(s, got):
        return lax.dot_general(
            s[...], got[...].reshape(256, 128), (((0,), (0,)), ((), ())), preferred_element_type=F32
        ).astype(BF)

    sent.append(back_a2[1]())
    proj[:, :128] = pick(slots, ta2r)
    sent.append(back_b2[1]())
    proj[:, 128:] = pick(slots_u, tb2r)
    proj_copy = pltpu.make_async_copy(proj, proj_o, out_sem.at[3])
    proj_copy.start()
    for copy in sent:
        copy.wait_send()
    for c in out_copies:
        c.wait()
    proj_copy.wait()


def body(
    grad_cot, grad_hidden, old_place, master, moment_one, moment_two, new_place, rows, dest, counts
):
    state = jax.ShapeDtypeStruct((1024, 128), F32)
    hbm = pl.BlockSpec(memory_space=pl.ANY)
    vmem = pl.BlockSpec(memory_space=pltpu.VMEM)
    smem = pl.BlockSpec(memory_space=pltpu.SMEM)
    v = lambda *s: pltpu.VMEM(s, BF)
    f = lambda *s: pltpu.VMEM(s, F32)
    scratch = [
        v(1024, 512), v(1024, 1024), v(128, 512),
        f(1024, 128), f(1024, 128), f(1024, 128), f(1024, 128), f(1024, 128), f(1024, 128),
        v(128, 256),
        v(512, 512), v(512, 512), v(512, 512), v(512, 512), v(256, 256), v(256, 256),
        v(128, 512), v(128, 512), v(256, 128), v(256, 128),
        v(8, 32, 512), v(8, 32, 512), v(16, 16, 512), v(16, 16, 512), v(4, 16, 16, 512), v(256, 2048),
        v(8, 64, 512), v(8, 64, 512), v(16, 32, 512), v(16, 32, 512),
        v(512, 512), v(16, 32, 512), v(16, 32, 512), v(8, 64, 512), v(8, 64, 512),
        v(4, 128, 128), v(4, 128, 128), v(4, 128, 128), v(4, 128, 128), v(32, 16, 128), v(32, 16, 128),
        v(8, 16, 16, 128), v(8, 16, 16, 128), v(16, 8, 16, 128), v(8, 16, 16, 128),
        v(8, 16, 16, 128), v(8, 16, 16, 128),
        v(16, 16, 128), v(8, 32, 128), v(16, 16, 128), v(8, 32, 128),
        v(8, 32, 128), v(16, 16, 128), v(8, 32, 128), v(16, 16, 128),
        pltpu.SemaphoreType.DMA((6,)), pltpu.SemaphoreType.DMA((4,)), pltpu.SemaphoreType.DMA((17,)),
        pltpu.SemaphoreType.DMA((17,)), pltpu.SemaphoreType.DMA((17,)),
    ]
    updated, first_new, second_new, projected = pl.pallas_call(
        kernel,
        out_shape=(state, state, state, jax.ShapeDtypeStruct((128, 256), BF)),
        in_specs=[hbm, hbm, vmem, hbm, hbm, hbm, smem, hbm, vmem, smem],
        out_specs=(hbm, hbm, hbm, hbm),
        scratch_shapes=scratch,
        compiler_params=pltpu.CompilerParams(
            collective_id=0, has_side_effects=True, vmem_limit_bytes=48 * 1024 * 1024
        ),
        name="whole_step",
    )(
        grad_cot, grad_hidden, old_place.reshape(1, 128), master.reshape(1024, 128),
        moment_one.reshape(1024, 128), moment_two.reshape(1024, 128), new_place, rows,
        dest.reshape(1, 128), counts,
    )
    back = lambda a: a.reshape(EXPERTS, 1, 4096)
    return (back(updated), back(first_new), back(second_new), projected)


def solution(mesh):
    return jax.shard_map(
        body,
        mesh=mesh,
        in_specs=(
            P("dp", "mp"),
            P("dp", None),
            P(),
            P(None, "mp", "dp"),
            P(None, "mp", "dp"),
            P(None, "mp", "dp"),
            P(),
            P("dp", "mp"),
            P("dp"),
            P("dp"),
        ),
        out_specs=(P(None, "mp", "dp"), P(None, "mp", "dp"), P(None, "mp", "dp"), P("dp", "mp")),
        check_vma=False,
    )
```

```python
import jax
import jax.numpy as jnp
from jax import lax
from jax.experimental import pallas as pl
from jax.experimental.pallas import tpu as pltpu
from jax.sharding import PartitionSpec as P

MESH = pl.DeviceIdType.MESH
BF = jnp.bfloat16
F32 = jnp.float32
I32 = jnp.int32

NY = 8
NU = 16
NX = 4
EXPERTS = 32

beta_first = 0.9
beta_second = 0.95
learn_rate = 0.01
decay_rate = 0.1
adam_eps = 1e-08
bias_first = 1.0 - 0.9**10
bias_second = 1.0 - 0.95**10


def adam_update(gradient, master, moment_one, moment_two):
    first_new = beta_first * moment_one + (1.0 - beta_first) * gradient
    second_new = beta_second * moment_two + (1.0 - beta_second) * gradient * gradient
    step_dir = first_new / bias_first / (jnp.sqrt(second_new / bias_second) + adam_eps)
    updated = master - learn_rate * (step_dir + decay_rate * master)
    return (updated, first_new, second_new)


def mm(a, b):
    return jnp.dot(a, b, preferred_element_type=F32)


def ones_where(cond):
    return jnp.where(cond, 1.0, 0.0).astype(BF)


def iota(shape, dim):
    return lax.broadcasted_iota(I32, shape, dim)


def swap_index(r, inner_bits, outer_bits, low_bits):
    low = r & ((1 << low_bits) - 1)
    outer = (r >> low_bits) & ((1 << outer_bits) - 1)
    inner = r >> (low_bits + outer_bits)
    return (((outer << inner_bits) | inner) << low_bits) | low


def reorder(first_bits, second_bits, low_bits):
    n = 1 << (first_bits + second_bits + low_bits)
    source = swap_index(iota((n, n), 0), second_bits, first_bits, low_bits)
    return ones_where(iota((n, n), 1) == source)


def kernel(
    cot_h, hid_h, old_ref, mas_h, one_h, two_h, new_s, rows_h, dest_ref, counts_s,
    mas_o, one_o, two_o, proj_o,
    cot, hid, rows, mas, one, two, mas_n, one_n, two_n, proj,
    p_a, p_at, p_c, p_ct, p_s, p_st, own_a, own_b, slots, slots_u,
    ra1, ra1r, ra2, ra2r, rb1, rb1r, rb2, rb2r, row, rowx, rowp,
    ga0, ga0r, ga1, ga1r, ha, ha0, ha0r, ha1, ha1r,
    gb0, gb0r, gb1, gb1r, hb, hb0, hb0r, hb1, hb1r,
    wa, wb, xa, xb, ya, yb, oa, ob, da0, da1, db0, db1, wea, web,
    ta1, tb1, ta1r, tb1r, ta2, tb2, ta2r, tb2r,
    in_sem, out_sem, loc_sem, snd_sem, rcv_sem,
):
    me = lax.axis_index("dp")
    mp = lax.axis_index("mp")
    y = me // NU
    u = lax.rem(me, NU)

    def peer_y(k):
        t = lax.rem(y + k, NY)
        return t, (t * NU + u, mp)

    def peer_u(k):
        t = lax.rem(u + k, NU)
        return t, (y * NU + t, mp)

    def peer_x(k):
        t = lax.rem(mp + k, NX)
        return t, (me, t)

    rings = {"y": (NY, y, peer_y), "u": (NU, u, peer_u), "x": (NX, mp, peer_x)}

    ins = [
        (cot_h, cot), (rows_h, rows), (mas_h, mas), (one_h, one), (two_h, two),
    ]
    for b in range(NX):
        at = pl.ds(b * 256, 256)
        ins.append((hid_h.at[:, at], hid.at[:, at]))
    in_copies = [pltpu.make_async_copy(s, d, in_sem.at[i]) for i, (s, d) in enumerate(ins)]
    for i in (1, 0, 5, 6, 7, 8, 2, 3, 4):
        in_copies[i].start()

    barrier = pltpu.get_barrier_semaphore()
    for n, _, peer in rings.values():

        @pl.loop(1, n)
        def _(k):
            pl.semaphore_signal(barrier, inc=1, device_id=peer(k)[1], device_id_type=MESH)

    def stage(i, ring, src, part, dst, place):
        n, mine, peer = rings[ring]

        def start():
            @pl.loop(1, n)
            def _(k):
                t, device = peer(k)
                pltpu.make_async_remote_copy(
                    src_ref=part(src, t), dst_ref=place(dst, mine), send_sem=snd_sem.at[i],
                    recv_sem=rcv_sem.at[i], device_id=device, device_id_type=MESH,
                ).start()

            pltpu.make_async_copy(part(src, mine), place(dst, mine), loc_sem.at[i]).start()

        return start

    def finish(i, ring, src_all, dst_all, src, part, dst, place):
        n, mine, peer = rings[ring]
        pltpu.make_async_copy(part(src, mine), place(dst, mine), loc_sem.at[i]).wait()
        whole = pltpu.make_async_remote_copy(
            src_ref=src_all(src, n - 1), dst_ref=dst_all(dst, n - 1), send_sem=snd_sem.at[i],
            recv_sem=rcv_sem.at[i], device_id=peer(1)[1], device_id_type=MESH,
        )
        whole.wait_recv()
        return whole

    lead = lambda ref, t: ref.at[t]
    lead_n = lambda ref, n: ref.at[pl.ds(0, n)]
    second = lambda ref, t: ref.at[:, t]
    second_n = lambda ref, n: ref.at[:, pl.ds(0, n)]
    whole_ref = lambda ref, t: ref

    def exchange(i, ring, src, dst, part=lead, place=lead):
        src_all = second_n if part is second else lead_n
        dst_all = second_n if place is second else lead_n
        if part is whole_ref:
            src_all = lambda ref, n: dst_all(dst, n)
        start = stage(i, ring, src, part, dst, place)
        wait = lambda: finish(i, ring, src_all, dst_all, src, part, dst, place)
        return start, wait

    rows_a1 = exchange(0, "y", ra1, ra1r)
    rows_a2 = exchange(1, "u", ra2, ra2r)
    rows_b1 = exchange(2, "u", rb1, rb1r)
    rows_b2 = exchange(3, "y", rb2, rb2r)
    rowsx = exchange(4, "x", row, rowx, part=whole_ref)
    grad_a = (exchange(5, "y", ga0, ga0r), exchange(6, "u", ga1, ga1r), exchange(7, "u", ha0, ha0r), exchange(8, "y", ha1, ha1r))
    grad_b = (exchange(9, "y", gb0, gb0r), exchange(10, "u", gb1, gb1r), exchange(11, "u", hb0, hb0r), exchange(12, "y", hb1, hb1r))
    cross_a = exchange(13, "x", wa, xa)
    cross_b = exchange(14, "x", wb, xb)
    back_a1 = exchange(15, "u", ta1, ta1r)
    back_a2 = exchange(16, "y", ta2, ta2r)
    back_b1 = exchange(17, "y", tb1, tb1r)
    back_b2 = exchange(18, "u", tb2, tb2r)
    sent = []

    z = u // 2
    core = lax.rem(u, 2)

    def remote(i, src, dst, device):
        return pltpu.make_async_remote_copy(
            src_ref=src, dst_ref=dst, send_sem=snd_sem.at[i], recv_sem=rcv_sem.at[i],
            device_id=device, device_id_type=MESH,
        )

    def to_core(i, which, part, place):
        def start():
            @pl.loop(1, NU // 2)
            def _(k):
                t = lax.rem(z + k, NU // 2)
                remote(i, part(t), place(u), (y * NU + t * 2 + which, mp)).start()

            @pl.when(core == which)
            def _():
                pltpu.make_async_copy(part(z), place(u), loc_sem.at[i]).start()

            @pl.when(core != which)
            def _():
                remote(i, part(z), place(u), (y * NU + z * 2 + which, mp)).start()

        def wait(gap):
            @pl.when(core == which)
            def _():
                pltpu.make_async_copy(part(z), place(u), loc_sem.at[i]).wait()
                remote(i, gap(NU - 1), gap(NU - 1), peer_u(1)[1]).wait_recv()

        def wait_send(gap):
            @pl.when(core == which)
            def _():
                remote(i, gap(NU // 2 - 1), gap(NU // 2 - 1), peer_u(1)[1]).wait_send()

            @pl.when(core != which)
            def _():
                remote(i, gap(NU // 2), gap(NU // 2), peer_u(1)[1]).wait_send()

        return start, wait, wait_send

    def along_y(i, part, place):
        def start():
            @pl.loop(1, NY)
            def _(k):
                t, device = peer_y(k)
                remote(i, part(t), place(y), device).start()

            pltpu.make_async_copy(part(y), place(y), loc_sem.at[i]).start()

        def wait(gap):
            pltpu.make_async_copy(part(y), place(y), loc_sem.at[i]).wait()
            remote(i, gap(NY - 1), gap(NY - 1), peer_y(1)[1]).wait_recv()

        def wait_send(gap):
            remote(i, gap(NY - 1), gap(NY - 1), peer_y(1)[1]).wait_send()

        return start, wait, wait_send

    def weight_path(i, out, d0, d1, got):
        first0 = to_core(i, 0, lambda t: out.at[:, t, 0], lambda s: d0.at[s])
        first1 = along_y(i + 1, lambda t: out.at[t, :, 1], lambda s: d1.at[s])
        then0 = along_y(i + 2, lambda t: d0.at[:, t], lambda s: got.at[s])
        then1 = to_core(i + 3, 1, lambda t: d1.at[:, t], lambda s: got.at[:, s])

        def first():
            first0[0]()
            first1[0]()

        def then():
            first0[1](lambda n: d0.at[pl.ds(0, n)])

            @pl.when(core == 0)
            def _():
                then0[0]()

            first1[1](lambda n: d1.at[pl.ds(0, n)])
            then1[0]()

        def last():
            @pl.when(core == 0)
            def _():
                then0[1](lambda n: got.at[pl.ds(0, n)])

            then1[1](lambda n: got.at[:, pl.ds(0, n)])

        def sends():
            first0[2](lambda n: d0.at[pl.ds(0, n)])
            first1[2](lambda n: d1.at[pl.ds(0, n)])

            @pl.when(core == 0)
            def _():
                then0[2](lambda n: got.at[pl.ds(0, n)])

            then1[2](lambda n: got.at[:, pl.ds(0, n)])

        return first, then, last, sends

    weight_a = weight_path(19, oa, da0, da1, wea)
    weight_b = weight_path(23, ob, db0, db1, web)

    dest = jnp.broadcast_to(dest_ref[...], (128, 128))
    dest_t = dest.astype(F32).T.astype(I32)
    earlier = (dest == dest_t) & (iota((128, 128), 0) < iota((128, 128), 1))
    rank = jnp.sum(jnp.where(earlier, 1, 0), axis=0, keepdims=True)
    dest_row = dest_ref[...]
    live = iota((1, 128), 1) < counts_s[0]
    slot_y = jnp.where(live, dest_row * 2 + rank, -1)
    slot_u = jnp.where(live, (dest_row & 15) * 16 + (dest_row >> 4) * 2 + rank, -1)
    slots[...] = ones_where(iota((256, 128), 0) == jnp.broadcast_to(slot_y, (256, 128)))
    slots_u[...] = ones_where(iota((256, 128), 0) == jnp.broadcast_to(slot_u, (256, 128)))
    in_copies[1].wait()
    ra1[...] = mm(slots[...], rows[:, :256]).astype(BF).reshape(NY, 32, 256)
    rb1[...] = mm(slots_u[...], rows[:, 256:]).astype(BF).reshape(NU, 16, 256)

    pl.semaphore_wait(barrier, NY - 1 + NU - 1 + NX - 1)
    rows_a1[0]()
    rows_b1[0]()
    p_a[...] = reorder(3, 4, 2)

    in_copies[0].wait()

    def partial(b):
        in_copies[5 + b].wait()
        return lax.dot_general(
            cot[...], hid[:, b * 256 : (b + 1) * 256], (((0,), (0,)), ((), ())), preferred_element_type=F32
        ).astype(BF)

    for b in range(2):
        lanes = slice(b * 128, (b + 1) * 128)
        part = partial(b)
        ga0[:, :, lanes] = part[:, :128].reshape(NY, 64, 128)
        gb0[:, :, lanes] = part[:, 128:].reshape(NY, 64, 128)
    grad_a[0][0]()
    for b in range(2):
        lanes = slice(b * 128, (b + 1) * 128)
        part = partial(2 + b)
        ha[:, lanes] = part[:, :128]
        hb[:, lanes] = part[:, 128:]
    ha0[...] = mm(p_a[...], ha[...]).astype(BF).reshape(NU, 32, 256)
    grad_a[2][0]()
    grad_b[0][0]()
    hb0[...] = mm(p_a[...], hb[...]).astype(BF).reshape(NU, 32, 256)
    grad_b[2][0]()

    p_at[...] = reorder(4, 3, 2)
    p_s[...] = reorder(3, 4, 1)
    p_st[...] = reorder(4, 3, 1)
    p_c[...] = reorder(2, 5, 2)
    p_ct[...] = reorder(5, 2, 2)
    old = jnp.broadcast_to(old_ref[...], (8, 128)).astype(F32).astype(BF)
    spread_b = ones_where(iota((128, 512), 0) == (iota((128, 512), 1) >> 2))
    col = iota((128, 512), 1)
    spread_a = ones_where(iota((128, 512), 0) == (((col >> 2) & 7) * NU + (col >> 5)))
    for spread, own in ((spread_a, own_a), (spread_b, own_b)):
        holder = mm(old, spread)[0:1].astype(I32)
        wanted = holder * 4 + (iota((1, 512), 1) & 3)
        own[...] = ones_where(iota((128, 512), 0) == jnp.broadcast_to(wanted, (128, 512)))

    sent.append(rows_a1[1]())
    ra2[...] = mm(p_s[...], ra1r[...].reshape(256, 256)).astype(BF).reshape(NU, 16, 256)
    sent.append(rows_b1[1]())
    rb2[...] = mm(p_st[...], rb1r[...].reshape(256, 256)).astype(BF).reshape(NY, 32, 256)

    def turn(grad, g0r, g1, h0r, h1):
        sent.append(grad[0][1]())
        g1[...] = mm(p_a[...], g0r[...].reshape(512, 256)).astype(BF).reshape(NU, 32, 256)
        grad[1][0]()
        sent.append(grad[2][1]())
        h1[...] = mm(p_at[...], h0r[...].reshape(512, 256)).astype(BF).reshape(NY, 64, 256)
        grad[3][0]()

    turn(grad_a, ga0r, ga1, ha0r, ha1)
    turn(grad_b, gb0r, gb1, hb0r, hb1)
    rows_a2[0]()
    rows_b2[0]()

    for i in (2, 3, 4):
        in_copies[i].wait()

    def step(grad, g1r, h1r, half, out, cross):
        for pair, own, recv, got in ((0, own_a, g1r, grad[1][1]), (2, own_b, h1r, grad[3][1])):
            sent.append(got())
            gradient = mm(own[...], recv[...].reshape(512, 256))
            for b in range(2):
                at = pl.ds(2 * (pair + b) + half, 128, stride=8)
                updated, first_new, second_new = adam_update(
                    gradient[:, b * 128 : (b + 1) * 128], mas[at, :], one[at, :], two[at, :]
                )
                mas_n[at, :] = updated
                one_n[at, :] = first_new
                two_n[at, :] = second_new
                out[pair + b] = updated.astype(BF)
        cross()

    def place_weights(got, x, table, out, start):
        sent.append(got())
        table[...] = mm(p_c[...], x[...].reshape(512, 128)).astype(BF).reshape(EXPERTS, 16, 128)

        @pl.loop(0, NY)
        def _(a):
            for b in range(NU):
                out[a, b // 2, b % 2] = table[new_s[a * NU + b]]

        start()

    step(grad_a, ga1r, ha1r, 0, wa, cross_a[0])
    place_weights(cross_a[1], xa, ya, oa, weight_a[0])
    step(grad_b, gb1r, hb1r, 1, wb, cross_b[0])
    outs = [(mas_n, mas_o), (one_n, one_o), (two_n, two_o), (proj, proj_o)]
    out_copies = [pltpu.make_async_copy(s, d, out_sem.at[i]) for i, (s, d) in enumerate(outs)]
    for c in out_copies[:3]:
        c.start()

    place_weights(cross_b[1], xb, yb, ob, weight_b[0])

    sent.append(rows_a2[1]())
    row[:, :, :256] = ra2r[...]
    sent.append(rows_b2[1]())
    row[:, :, 256:] = mm(p_s[...], rb2r[...].reshape(256, 256)).astype(BF).reshape(NU, 16, 256)
    rowsx[0]()
    weight_a[1]()
    weight_b[1]()
    sent.append(rowsx[1]())
    for b in range(4):
        lanes = jnp.concatenate(
            [rowx[m, :, :, b * 128 : (b + 1) * 128].reshape(256, 128) for m in range(NX)], axis=1
        )
        rowp[:, b * 512 : (b + 1) * 512] = mm(lanes, p_ct[...]).astype(BF)

    weight_a[2]()
    out_a = mm(rowp[...], wea[...].reshape(2048, 128)).astype(BF)
    ta1[...] = out_a.reshape(NU, 16, 128)
    back_a1[0]()
    weight_b[2]()
    out_b = mm(rowp[...], web[...].reshape(2048, 128)).astype(BF)
    tb1[...] = mm(p_st[...], out_b).astype(BF).reshape(NY, 32, 128)
    back_b1[0]()
    sent.append(back_a1[1]())
    ta2[...] = mm(p_st[...], ta1r[...].reshape(256, 128)).astype(BF).reshape(NY, 32, 128)
    back_a2[0]()
    sent.append(back_b1[1]())
    tb2[...] = mm(p_s[...], tb1r[...].reshape(256, 128)).astype(BF).reshape(NU, 16, 128)
    back_b2[0]()

    def pick(s, got):
        return lax.dot_general(
            s[...], got[...].reshape(256, 128), (((0,), (0,)), ((), ())), preferred_element_type=F32
        ).astype(BF)

    sent.append(back_a2[1]())
    proj[:, :128] = pick(slots, ta2r)
    sent.append(back_b2[1]())
    proj[:, 128:] = pick(slots_u, tb2r)
    out_copies[3].start()
    for copy in sent:
        copy.wait_send()
    weight_a[3]()
    weight_b[3]()
    for c in out_copies:
        c.wait()


def commit(a, b, c, d, a_o, b_o, c_o, d_o, a_v, b_v, c_v, d_v, sem):
    moves = ((d, d_v, d_o), (a, a_v, a_o), (b, b_v, b_o), (c, c_v, c_o))
    gets = [pltpu.make_async_copy(x, v, sem.at[i]) for i, (x, v, _) in enumerate(moves)]
    puts = [pltpu.make_async_copy(v, o, sem.at[4 + i]) for i, (_, v, o) in enumerate(moves)]
    for get in gets:
        get.start()
    for get, put in zip(gets, puts):
        get.wait()
        put.start()
    for put in puts:
        put.wait()


def body(
    grad_cot, grad_hidden, old_place, master, moment_one, moment_two, new_place, rows, dest, counts
):
    state = jax.ShapeDtypeStruct((1024, 128), F32)
    hbm = pl.BlockSpec(memory_space=pltpu.HBM)
    vmem = pl.BlockSpec(memory_space=pltpu.VMEM)
    smem = pl.BlockSpec(memory_space=pltpu.SMEM)
    v = lambda *s: pltpu.VMEM(s, BF)
    f = lambda *s: pltpu.VMEM(s, F32)
    scratch = [
        v(1024, 512), v(1024, 1024), v(128, 512),
        f(1024, 128), f(1024, 128), f(1024, 128), f(1024, 128), f(1024, 128), f(1024, 128),
        v(128, 256),
        v(512, 512), v(512, 512), v(512, 512), v(512, 512), v(256, 256), v(256, 256),
        v(128, 512), v(128, 512), v(256, 128), v(256, 128),
        v(8, 32, 256), v(8, 32, 256), v(16, 16, 256), v(16, 16, 256),
        v(16, 16, 256), v(16, 16, 256), v(8, 32, 256), v(8, 32, 256),
        v(16, 16, 512), v(4, 16, 16, 512), v(256, 2048),
        v(8, 64, 256), v(8, 64, 256), v(16, 32, 256), v(16, 32, 256),
        v(512, 256), v(16, 32, 256), v(16, 32, 256), v(8, 64, 256), v(8, 64, 256),
        v(8, 64, 256), v(8, 64, 256), v(16, 32, 256), v(16, 32, 256),
        v(512, 256), v(16, 32, 256), v(16, 32, 256), v(8, 64, 256), v(8, 64, 256),
        v(4, 128, 128), v(4, 128, 128), v(4, 128, 128), v(4, 128, 128), v(32, 16, 128), v(32, 16, 128),
        v(8, 8, 2, 16, 128), v(8, 8, 2, 16, 128),
        v(16, 8, 16, 128), v(8, 8, 16, 128), v(16, 8, 16, 128), v(8, 8, 16, 128),
        v(8, 16, 16, 128), v(8, 16, 16, 128),
        v(16, 16, 128), v(8, 32, 128), v(16, 16, 128), v(8, 32, 128),
        v(8, 32, 128), v(16, 16, 128), v(8, 32, 128), v(16, 16, 128),
        pltpu.SemaphoreType.DMA((9,)), pltpu.SemaphoreType.DMA((4,)), pltpu.SemaphoreType.DMA((27,)),
        pltpu.SemaphoreType.DMA((27,)), pltpu.SemaphoreType.DMA((27,)),
    ]
    shapes = (state, state, state, jax.ShapeDtypeStruct((128, 256), BF))
    results = pl.pallas_call(
        kernel,
        out_shape=shapes,
        in_specs=[hbm, hbm, vmem, hbm, hbm, hbm, smem, hbm, vmem, smem],
        out_specs=(hbm,) * 4,
        scratch_shapes=scratch,
        compiler_params=pltpu.CompilerParams(
            collective_id=0, has_side_effects=True, vmem_limit_bytes=67043328
        ),
        name="whole_step",
    )(
        grad_cot, grad_hidden, old_place.reshape(1, 128), master.reshape(1024, 128),
        moment_one.reshape(1024, 128), moment_two.reshape(1024, 128), new_place, rows,
        dest.reshape(1, 128), counts,
    )
    updated, first_new, second_new, projected = pl.pallas_call(
        commit,
        out_shape=shapes,
        in_specs=[hbm] * 4,
        out_specs=(hbm,) * 4,
        scratch_shapes=[f(1024, 128), f(1024, 128), f(1024, 128), v(128, 256), pltpu.SemaphoreType.DMA((8,))],
        compiler_params=pltpu.CompilerParams(vmem_limit_bytes=67043328),
        name="commit",
    )(*results)
    back = lambda a: a.reshape(EXPERTS, 1, 4096)
    return (back(updated), back(first_new), back(second_new), projected)


def solution(mesh):
    return jax.shard_map(
        body,
        mesh=mesh,
        in_specs=(
            P("dp", "mp"),
            P("dp", None),
            P(),
            P(None, "mp", "dp"),
            P(None, "mp", "dp"),
            P(None, "mp", "dp"),
            P(),
            P("dp", "mp"),
            P("dp"),
            P("dp"),
        ),
        out_specs=(P(None, "mp", "dp"), P(None, "mp", "dp"), P(None, "mp", "dp"), P("dp", "mp")),
        check_vma=False,
    )
```

```python
import jax
import jax.numpy as jnp
from jax import lax
from jax.experimental import pallas as pl
from jax.experimental.pallas import tpu as pltpu
from jax.sharding import PartitionSpec as P

MESH = pl.DeviceIdType.MESH
BF = jnp.bfloat16
F32 = jnp.float32
I32 = jnp.int32

NY = 8
NU = 16
NX = 4
EXPERTS = 32

beta_first = 0.9
beta_second = 0.95
learn_rate = 0.01
decay_rate = 0.1
adam_eps = 1e-08
bias_first = 1.0 - 0.9**10
bias_second = 1.0 - 0.95**10


def adam_update(gradient, master, moment_one, moment_two):
    first_new = beta_first * moment_one + (1.0 - beta_first) * gradient
    second_new = beta_second * moment_two + (1.0 - beta_second) * gradient * gradient
    step_dir = first_new / bias_first / (jnp.sqrt(second_new / bias_second) + adam_eps)
    updated = master - learn_rate * (step_dir + decay_rate * master)
    return (updated, first_new, second_new)


def mm(a, b):
    return jnp.dot(a, b, preferred_element_type=F32)


def ones_where(cond):
    return jnp.where(cond, 1.0, 0.0).astype(BF)


def iota(shape, dim):
    return lax.broadcasted_iota(I32, shape, dim)


def swap_index(r, inner_bits, outer_bits, low_bits):
    low = r & ((1 << low_bits) - 1)
    outer = (r >> low_bits) & ((1 << outer_bits) - 1)
    inner = r >> (low_bits + outer_bits)
    return (((outer << inner_bits) | inner) << low_bits) | low


def reorder(first_bits, second_bits, low_bits):
    n = 1 << (first_bits + second_bits + low_bits)
    source = swap_index(iota((n, n), 0), second_bits, first_bits, low_bits)
    return ones_where(iota((n, n), 1) == source)


def kernel(
    cot_h, hid_h, old_h, mas_h, one_h, two_h, new_s, rows_h, dest_h, counts_s,
    mas_n, one_n, two_n, proj,
    cot, cot_t, hid, rows, mas, one, two, old_ref, dest_ref,
    p_a, p_at, p_c, p_ct, p_s, p_st, own_a, own_b, slots, slots_u,
    ra1, ra1r, ra2, ra2r, rb1, rb1r, rb2, rb2r, row, rowx, rowp, rowq,
    ga0, ga0r, ga1, ga1r, ha, ha0, ha0r, ha1, ha1r,
    gb0, gb0r, gb1, gb1r, hb, hb0, hb0r, hb1, hb1r,
    wa, wb, xa, xb, ya, yb, oa, ob, da0, da1, db0, db1, wea, web,
    ta1, tb1, ta1r, tb1r, ta2, tb2, ta2r, tb2r,
    in_sem, loc_sem, snd_sem, rcv_sem,
):
    me = lax.axis_index("dp")
    mp = lax.axis_index("mp")
    y = me // NU
    u = lax.rem(me, NU)

    def peer_y(k):
        t = lax.rem(y + k, NY)
        return t, (t * NU + u, mp)

    def peer_u(k):
        t = lax.rem(u + k, NU)
        return t, (y * NU + t, mp)

    def peer_x(k):
        t = lax.rem(mp + k, NX)
        return t, (me, t)

    def hop(k, n):
        return n // 2 + lax.rem(k + 1, 2) * (k // 2) - lax.rem(k, 2) * (k // 2)

    rings = {"y": (NY, y, peer_y), "u": (NU, u, peer_u), "x": (NX, mp, peer_x)}

    ins = [
        (cot_h, cot), (rows_h, rows), (mas_h, mas), (one_h, one), (two_h, two),
    ]
    for b in range(NX):
        at = pl.ds(b * 256, 256)
        ins.append((hid_h.at[:, at], hid.at[:, at]))
    ins += [(dest_h, dest_ref), (old_h, old_ref)]
    in_copies = [pltpu.make_async_copy(s, d, in_sem.at[i]) for i, (s, d) in enumerate(ins)]
    for i in (9, 1, 0, 5, 6, 7, 8, 10, 2, 3, 4):
        in_copies[i].start()

    barrier = pltpu.get_barrier_semaphore()
    for n, _, peer in rings.values():

        @pl.loop(1, n)
        def _(k):
            pl.semaphore_signal(barrier, inc=1, device_id=peer(k)[1], device_id_type=MESH)

    def stage(i, ring, src, part, dst, place):
        n, mine, peer = rings[ring]

        def start():
            @pl.loop(1, n)
            def _(k):
                t, device = peer(hop(k, n))
                pltpu.make_async_remote_copy(
                    src_ref=part(src, t), dst_ref=place(dst, mine), send_sem=snd_sem.at[i],
                    recv_sem=rcv_sem.at[i], device_id=device, device_id_type=MESH,
                ).start()

            pltpu.make_async_copy(part(src, mine), place(dst, mine), loc_sem.at[i]).start()

        return start

    def finish(i, ring, src_all, dst_all, src, part, dst, place):
        n, mine, peer = rings[ring]
        pltpu.make_async_copy(part(src, mine), place(dst, mine), loc_sem.at[i]).wait()
        whole = pltpu.make_async_remote_copy(
            src_ref=src_all(src, n - 1), dst_ref=dst_all(dst, n - 1), send_sem=snd_sem.at[i],
            recv_sem=rcv_sem.at[i], device_id=peer(1)[1], device_id_type=MESH,
        )
        whole.wait_recv()
        return whole

    lead = lambda ref, t: ref.at[t]
    lead_n = lambda ref, n: ref.at[pl.ds(0, n)]
    second = lambda ref, t: ref.at[:, t]
    second_n = lambda ref, n: ref.at[:, pl.ds(0, n)]
    whole_ref = lambda ref, t: ref

    def exchange(i, ring, src, dst, part=lead, place=lead):
        src_all = second_n if part is second else lead_n
        dst_all = second_n if place is second else lead_n
        if part is whole_ref:
            src_all = lambda ref, n: dst_all(dst, n)
        start = stage(i, ring, src, part, dst, place)
        wait = lambda: finish(i, ring, src_all, dst_all, src, part, dst, place)
        return start, wait

    rows_a1 = exchange(0, "y", ra1, ra1r)
    rows_a2 = exchange(1, "u", ra2, ra2r)
    rows_b1 = exchange(2, "u", rb1, rb1r)
    rows_b2 = exchange(3, "y", rb2, rb2r)
    rowsx = exchange(4, "x", row, rowx, part=whole_ref)
    grad_a = (exchange(5, "y", ga0, ga0r), exchange(6, "u", ga1, ga1r), exchange(7, "u", ha0, ha0r), exchange(8, "y", ha1, ha1r))
    grad_b = (exchange(9, "y", gb0, gb0r), exchange(10, "u", gb1, gb1r), exchange(11, "u", hb0, hb0r), exchange(12, "y", hb1, hb1r))
    cross_a = exchange(13, "x", wa, xa)
    cross_b = exchange(14, "x", wb, xb)
    back_a1 = exchange(15, "u", ta1, ta1r)
    back_a2 = exchange(16, "y", ta2, ta2r)
    back_b1 = exchange(17, "y", tb1, tb1r)
    back_b2 = exchange(18, "u", tb2, tb2r)
    sent = []

    z = u // 2
    core = lax.rem(u, 2)

    def remote(i, src, dst, device):
        return pltpu.make_async_remote_copy(
            src_ref=src, dst_ref=dst, send_sem=snd_sem.at[i], recv_sem=rcv_sem.at[i],
            device_id=device, device_id_type=MESH,
        )

    def to_core(i, which, part, place):
        def start():
            @pl.loop(1, NU // 2)
            def _(k):
                t = lax.rem(z + hop(k, NU // 2), NU // 2)
                remote(i, part(t), place(u), (y * NU + t * 2 + which, mp)).start()

            @pl.when(core == which)
            def _():
                pltpu.make_async_copy(part(z), place(u), loc_sem.at[i]).start()

            @pl.when(core != which)
            def _():
                remote(i, part(z), place(u), (y * NU + z * 2 + which, mp)).start()

        def wait(gap):
            @pl.when(core == which)
            def _():
                pltpu.make_async_copy(part(z), place(u), loc_sem.at[i]).wait()
                remote(i, gap(NU - 1), gap(NU - 1), peer_u(1)[1]).wait_recv()

        def wait_send(gap):
            @pl.when(core == which)
            def _():
                remote(i, gap(NU // 2 - 1), gap(NU // 2 - 1), peer_u(1)[1]).wait_send()

            @pl.when(core != which)
            def _():
                remote(i, gap(NU // 2), gap(NU // 2), peer_u(1)[1]).wait_send()

        return start, wait, wait_send

    def along_y(i, part, place):
        def start():
            @pl.loop(1, NY)
            def _(k):
                t, device = peer_y(hop(k, NY))
                remote(i, part(t), place(y), device).start()

            pltpu.make_async_copy(part(y), place(y), loc_sem.at[i]).start()

        def wait(gap):
            pltpu.make_async_copy(part(y), place(y), loc_sem.at[i]).wait()
            remote(i, gap(NY - 1), gap(NY - 1), peer_y(1)[1]).wait_recv()

        def wait_send(gap):
            remote(i, gap(NY - 1), gap(NY - 1), peer_y(1)[1]).wait_send()

        return start, wait, wait_send

    def weight_path(i, out, d0, d1, got):
        first0 = to_core(i, 0, lambda t: out.at[:, t, 0], lambda s: d0.at[s])
        first1 = along_y(i + 1, lambda t: out.at[t, :, 1], lambda s: d1.at[s])
        then0 = along_y(i + 2, lambda t: d0.at[:, t], lambda s: got.at[s])
        then1 = to_core(i + 3, 1, lambda t: d1.at[:, t], lambda s: got.at[:, s])

        def first():
            first0[0]()
            first1[0]()

        def then():
            first0[1](lambda n: d0.at[pl.ds(0, n)])

            @pl.when(core == 0)
            def _():
                then0[0]()

            first1[1](lambda n: d1.at[pl.ds(0, n)])
            then1[0]()

        def last():
            @pl.when(core == 0)
            def _():
                then0[1](lambda n: got.at[pl.ds(0, n)])

            then1[1](lambda n: got.at[:, pl.ds(0, n)])

        def sends():
            first0[2](lambda n: d0.at[pl.ds(0, n)])
            first1[2](lambda n: d1.at[pl.ds(0, n)])

            @pl.when(core == 0)
            def _():
                then0[2](lambda n: got.at[pl.ds(0, n)])

            then1[2](lambda n: got.at[:, pl.ds(0, n)])

        return first, then, last, sends

    weight_a = weight_path(19, oa, da0, da1, wea)
    weight_b = weight_path(23, ob, db0, db1, web)

    in_copies[9].wait()

    dest = jnp.broadcast_to(dest_ref[...], (128, 128))
    dest_t = dest.astype(F32).T.astype(I32)
    earlier = (dest == dest_t) & (iota((128, 128), 0) < iota((128, 128), 1))
    rank = jnp.sum(jnp.where(earlier, 1, 0), axis=0, keepdims=True)
    dest_row = dest_ref[...]
    live = iota((1, 128), 1) < counts_s[0]
    slot_y = jnp.where(live, dest_row * 2 + rank, -1)
    slot_u = jnp.where(live, (dest_row & 15) * 16 + (dest_row >> 4) * 2 + rank, -1)
    slots[...] = ones_where(iota((256, 128), 0) == jnp.broadcast_to(slot_y, (256, 128)))
    slots_u[...] = ones_where(iota((256, 128), 0) == jnp.broadcast_to(slot_u, (256, 128)))
    in_copies[1].wait()
    ra1[...] = mm(slots[...], rows[:, :256]).astype(BF).reshape(NY, 32, 256)
    rb1[...] = mm(slots_u[...], rows[:, 256:]).astype(BF).reshape(NU, 16, 256)

    pl.semaphore_wait(barrier, NY - 1 + NU - 1 + NX - 1)
    rows_a1[0]()
    rows_b1[0]()
    p_a[...] = reorder(3, 4, 2)

    in_copies[0].wait()
    cot_t[...] = cot[...].T

    def partial(b):
        in_copies[5 + b].wait()
        return mm(cot_t[...], hid[:, b * 256 : (b + 1) * 256]).astype(BF)

    for b in range(2):
        lanes = slice(b * 128, (b + 1) * 128)
        part = partial(b)
        ga0[:, :, lanes] = part[:, :128].reshape(NY, 64, 128)
        gb0[:, :, lanes] = part[:, 128:].reshape(NY, 64, 128)
    grad_a[0][0]()
    for b in range(2):
        lanes = slice(b * 128, (b + 1) * 128)
        part = partial(2 + b)
        ha[:, lanes] = part[:, :128]
        hb[:, lanes] = part[:, 128:]
    ha0[...] = mm(p_a[...], ha[...]).astype(BF).reshape(NU, 32, 256)
    grad_a[2][0]()
    grad_b[0][0]()
    hb0[...] = mm(p_a[...], hb[...]).astype(BF).reshape(NU, 32, 256)
    grad_b[2][0]()

    p_at[...] = reorder(4, 3, 2)
    p_s[...] = reorder(3, 4, 1)
    p_st[...] = reorder(4, 3, 1)
    p_c[...] = reorder(2, 5, 2)
    p_ct[...] = reorder(5, 2, 2)
    in_copies[10].wait()
    old = jnp.broadcast_to(old_ref[...], (8, 128)).astype(F32).astype(BF)
    spread_b = ones_where(iota((128, 512), 0) == (iota((128, 512), 1) >> 2))
    col = iota((128, 512), 1)
    spread_a = ones_where(iota((128, 512), 0) == (((col >> 2) & 7) * NU + (col >> 5)))
    for spread, own in ((spread_a, own_a), (spread_b, own_b)):
        holder = mm(old, spread)[0:1].astype(I32)
        wanted = holder * 4 + (iota((1, 512), 1) & 3)
        own[...] = ones_where(iota((128, 512), 0) == jnp.broadcast_to(wanted, (128, 512)))

    sent.append(rows_a1[1]())
    ra2[...] = mm(p_s[...], ra1r[...].reshape(256, 256)).astype(BF).reshape(NU, 16, 256)
    sent.append(rows_b1[1]())
    rb2[...] = mm(p_st[...], rb1r[...].reshape(256, 256)).astype(BF).reshape(NY, 32, 256)

    def turn(grad, g0r, g1, h0r, h1):
        sent.append(grad[0][1]())
        g1[...] = mm(p_a[...], g0r[...].reshape(512, 256)).astype(BF).reshape(NU, 32, 256)
        grad[1][0]()
        sent.append(grad[2][1]())
        h1[...] = mm(p_at[...], h0r[...].reshape(512, 256)).astype(BF).reshape(NY, 64, 256)
        grad[3][0]()

    turn(grad_a, ga0r, ga1, ha0r, ha1)
    turn(grad_b, gb0r, gb1, hb0r, hb1)
    rows_a2[0]()
    rows_b2[0]()

    for i in (2, 3, 4):
        in_copies[i].wait()

    def step(grad, g1r, h1r, half, out, cross):
        for pair, own, recv, got in ((0, own_a, g1r, grad[1][1]), (2, own_b, h1r, grad[3][1])):
            sent.append(got())
            gradient = mm(own[...], recv[...].reshape(512, 256))
            for b in range(2):
                at = pl.ds(2 * (pair + b) + half, 128, stride=8)
                updated, first_new, second_new = adam_update(
                    gradient[:, b * 128 : (b + 1) * 128], mas[at, :], one[at, :], two[at, :]
                )
                mas_n[at, :] = updated
                one_n[at, :] = first_new
                two_n[at, :] = second_new
                out[pair + b] = updated.astype(BF)
        cross()

    def place_weights(got, x, table, out, start):
        sent.append(got())
        table[...] = mm(p_c[...], x[...].reshape(512, 128)).astype(BF).reshape(EXPERTS, 16, 128)

        @pl.loop(0, NY)
        def _(a):
            for b in range(NU):
                out[a, b // 2, b % 2] = table[new_s[a * NU + b]]

        start()

    step(grad_a, ga1r, ha1r, 0, wa, cross_a[0])
    place_weights(cross_a[1], xa, ya, oa, weight_a[0])
    step(grad_b, gb1r, hb1r, 1, wb, cross_b[0])
    place_weights(cross_b[1], xb, yb, ob, weight_b[0])

    sent.append(rows_a2[1]())
    row[:, :, :256] = ra2r[...]
    sent.append(rows_b2[1]())
    row[:, :, 256:] = mm(p_s[...], rb2r[...].reshape(256, 256)).astype(BF).reshape(NU, 16, 256)
    rowsx[0]()
    weight_a[1]()
    weight_b[1]()
    sent.append(rowsx[1]())
    for b in range(4):
        lanes = jnp.concatenate(
            [rowx[m, :, :, b * 128 : (b + 1) * 128].reshape(256, 128) for m in range(NX)], axis=1
        )
        turned = mm(lanes, p_ct[...]).astype(BF)
        rowp[:, b * 512 : (b + 1) * 512] = turned
        rowq[:, b * 512 : (b + 1) * 512] = mm(p_st[...], turned).astype(BF)

    weight_a[2]()
    out_a = mm(rowp[...], wea[...].reshape(2048, 128)).astype(BF)
    ta1[...] = out_a.reshape(NU, 16, 128)
    back_a1[0]()
    weight_b[2]()
    out_b = mm(rowq[...], web[...].reshape(2048, 128)).astype(BF)
    tb1[...] = out_b.reshape(NY, 32, 128)
    back_b1[0]()
    sent.append(back_a1[1]())
    ta2[...] = mm(p_st[...], ta1r[...].reshape(256, 128)).astype(BF).reshape(NY, 32, 128)
    back_a2[0]()
    sent.append(back_b1[1]())
    tb2[...] = mm(p_s[...], tb1r[...].reshape(256, 128)).astype(BF).reshape(NU, 16, 128)
    back_b2[0]()

    def pick(s, got):
        return lax.dot_general(
            s[...], got[...].reshape(256, 128), (((0,), (0,)), ((), ())), preferred_element_type=F32
        ).astype(BF)

    sent.append(back_a2[1]())
    proj[:, :128] = pick(slots, ta2r)
    sent.append(back_b2[1]())
    proj[:, 128:] = pick(slots_u, tb2r)
    for copy in sent:
        copy.wait_send()
    weight_a[3]()
    weight_b[3]()


def commit(a, b, c, d, a_o, b_o, c_o, d_o, sem):
    moves = ((a, a_o), (b, b_o), (c, c_o), (d, d_o))
    puts = [pltpu.make_async_copy(v, o, sem.at[i]) for i, (v, o) in enumerate(moves)]
    for put in puts:
        put.start()
    for put in puts:
        put.wait()


def body(
    grad_cot, grad_hidden, old_place, master, moment_one, moment_two, new_place, rows, dest, counts
):
    state = jax.ShapeDtypeStruct((1024, 128), F32)
    hbm = pl.BlockSpec(memory_space=pltpu.HBM)
    vmem = pl.BlockSpec(memory_space=pltpu.VMEM)
    smem = pl.BlockSpec(memory_space=pltpu.SMEM)
    pin = lambda x: pltpu.with_memory_space_constraint(x, pltpu.HBM)
    v = lambda *s: pltpu.VMEM(s, BF)
    f = lambda *s: pltpu.VMEM(s, F32)
    scratch = [
        v(1024, 512), v(512, 1024), v(1024, 1024), v(128, 512),
        f(1024, 128), f(1024, 128), f(1024, 128), pltpu.VMEM((1, 128), I32), pltpu.VMEM((1, 128), I32),
        v(512, 512), v(512, 512), v(512, 512), v(512, 512), v(256, 256), v(256, 256),
        v(128, 512), v(128, 512), v(256, 128), v(256, 128),
        v(8, 32, 256), v(8, 32, 256), v(16, 16, 256), v(16, 16, 256),
        v(16, 16, 256), v(16, 16, 256), v(8, 32, 256), v(8, 32, 256),
        v(16, 16, 512), v(4, 16, 16, 512), v(256, 2048), v(256, 2048),
        v(8, 64, 256), v(8, 64, 256), v(16, 32, 256), v(16, 32, 256),
        v(512, 256), v(16, 32, 256), v(16, 32, 256), v(8, 64, 256), v(8, 64, 256),
        v(8, 64, 256), v(8, 64, 256), v(16, 32, 256), v(16, 32, 256),
        v(512, 256), v(16, 32, 256), v(16, 32, 256), v(8, 64, 256), v(8, 64, 256),
        v(4, 128, 128), v(4, 128, 128), v(4, 128, 128), v(4, 128, 128), v(32, 16, 128), v(32, 16, 128),
        v(8, 8, 2, 16, 128), v(8, 8, 2, 16, 128),
        v(16, 8, 16, 128), v(8, 8, 16, 128), v(16, 8, 16, 128), v(8, 8, 16, 128),
        v(8, 16, 16, 128), v(8, 16, 16, 128),
        v(16, 16, 128), v(8, 32, 128), v(16, 16, 128), v(8, 32, 128),
        v(8, 32, 128), v(16, 16, 128), v(8, 32, 128), v(16, 16, 128),
        pltpu.SemaphoreType.DMA((11,)), pltpu.SemaphoreType.DMA((27,)),
        pltpu.SemaphoreType.DMA((27,)), pltpu.SemaphoreType.DMA((27,)),
    ]
    shapes = (state, state, state, jax.ShapeDtypeStruct((128, 256), BF))
    results = pl.pallas_call(
        kernel,
        out_shape=shapes,
        in_specs=[hbm, hbm, hbm, hbm, hbm, hbm, smem, hbm, hbm, smem],
        out_specs=(vmem,) * 4,
        scratch_shapes=scratch,
        compiler_params=pltpu.CompilerParams(
            collective_id=0, has_side_effects=True, vmem_limit_bytes=50331648
        ),
        name="whole_step",
    )(
        pin(grad_cot), pin(grad_hidden), pin(old_place.reshape(1, 128)), pin(master.reshape(1024, 128)),
        pin(moment_one.reshape(1024, 128)), pin(moment_two.reshape(1024, 128)), pin(new_place), pin(rows),
        pin(dest.reshape(1, 128)), counts,
    )
    updated, first_new, second_new, projected = pl.pallas_call(
        commit,
        out_shape=shapes,
        in_specs=[vmem] * 4,
        out_specs=(hbm,) * 4,
        scratch_shapes=[pltpu.SemaphoreType.DMA((4,))],
        compiler_params=pltpu.CompilerParams(vmem_limit_bytes=1048576),
        name="commit",
    )(*results)
    back = lambda a: a.reshape(EXPERTS, 1, 4096)
    return (back(updated), back(first_new), back(second_new), projected)


def solution(mesh):
    return jax.shard_map(
        body,
        mesh=mesh,
        in_specs=(
            P("dp", "mp"),
            P("dp", None),
            P(),
            P(None, "mp", "dp"),
            P(None, "mp", "dp"),
            P(None, "mp", "dp"),
            P(),
            P("dp", "mp"),
            P("dp"),
            P("dp"),
        ),
        out_specs=(P(None, "mp", "dp"), P(None, "mp", "dp"), P(None, "mp", "dp"), P("dp", "mp")),
        check_vma=False,
    )
```

```python
import jax
import jax.numpy as jnp
from jax import lax
from jax.experimental import pallas as pl
from jax.experimental.pallas import tpu as pltpu
from jax.sharding import PartitionSpec as P

MESH = pl.DeviceIdType.MESH
BF = jnp.bfloat16
F32 = jnp.float32
I32 = jnp.int32

NY = 8
NU = 16
NX = 4
EXPERTS = 32

beta_first = 0.9
beta_second = 0.95
learn_rate = 0.01
decay_rate = 0.1
adam_eps = 1e-08
bias_first = 1.0 - 0.9**10
bias_second = 1.0 - 0.95**10


def adam_update(gradient, master, moment_one, moment_two):
    first_new = beta_first * moment_one + (1.0 - beta_first) * gradient
    second_new = beta_second * moment_two + (1.0 - beta_second) * gradient * gradient
    step_dir = first_new / bias_first / (jnp.sqrt(second_new / bias_second) + adam_eps)
    updated = master - learn_rate * (step_dir + decay_rate * master)
    return (updated, first_new, second_new)


def mm(a, b):
    return jnp.dot(a, b, preferred_element_type=F32)


def ones_where(cond):
    return jnp.where(cond, 1.0, 0.0).astype(BF)


def iota(shape, dim):
    return lax.broadcasted_iota(I32, shape, dim)


def swap_index(r, inner_bits, outer_bits, low_bits):
    low = r & ((1 << low_bits) - 1)
    outer = (r >> low_bits) & ((1 << outer_bits) - 1)
    inner = r >> (low_bits + outer_bits)
    return (((outer << inner_bits) | inner) << low_bits) | low


def reorder(first_bits, second_bits, low_bits):
    n = 1 << (first_bits + second_bits + low_bits)
    source = swap_index(iota((n, n), 0), second_bits, first_bits, low_bits)
    return ones_where(iota((n, n), 1) == source)


def kernel(
    cot_h, hid_h, old_h, mas_h, one_h, two_h, new_s, rows_h, dest_h, counts_s,
    mas_n, one_n, two_n, proj,
    cot, hid, rows, mas, one, two, old_ref, dest_ref,
    p_a, p_at, p_c, p_ct, p_s, p_st, own_a, own_b, slots, slots_u,
    ra1, ra1r, ra2, ra2r, rb1, rb1r, rb2, rb2r, row, rowx, rowp, rowq,
    ga0, ga0r, ga1, ga1r, ha, ha0, ha0r, ha1, ha1r,
    gb0, gb0r, gb1, gb1r, hb, hb0, hb0r, hb1, hb1r,
    wa, wb, xa, xb, ya, yb, oa, ob, da0, da1, db0, db1, wea, web,
    ta1, tb1, ta1r, tb1r, ta2, tb2, ta2r, tb2r,
    in_sem, loc_sem, snd_sem, rcv_sem,
):
    me = lax.axis_index("dp")
    mp = lax.axis_index("mp")
    y = me // NU
    u = lax.rem(me, NU)

    def peer_y(k):
        t = lax.rem(y + k, NY)
        return t, (t * NU + u, mp)

    def peer_u(k):
        t = lax.rem(u + k, NU)
        return t, (y * NU + t, mp)

    def peer_x(k):
        t = lax.rem(mp + k, NX)
        return t, (me, t)

    def hop(k, n):
        return n // 2 + lax.rem(k + 1, 2) * (k // 2) - lax.rem(k, 2) * (k // 2)

    rings = {"y": (NY, y, peer_y), "u": (NU, u, peer_u), "x": (NX, mp, peer_x)}

    ins = [
        (cot_h, cot), (rows_h, rows), (mas_h, mas), (one_h, one), (two_h, two),
    ]
    for b in range(NX):
        at = pl.ds(b * 256, 256)
        ins.append((hid_h.at[:, at], hid.at[:, at]))
    ins += [(dest_h, dest_ref), (old_h, old_ref)]
    in_copies = [pltpu.make_async_copy(s, d, in_sem.at[i]) for i, (s, d) in enumerate(ins)]
    for i in (9, 1, 0, 5, 6, 7, 8, 10, 2, 3, 4):
        in_copies[i].start()

    barrier = pltpu.get_barrier_semaphore()
    for n, _, peer in rings.values():

        @pl.loop(1, n)
        def _(k):
            pl.semaphore_signal(barrier, inc=1, device_id=peer(k)[1], device_id_type=MESH)

    def stage(i, ring, src, part, dst, place):
        n, mine, peer = rings[ring]

        def start():
            @pl.loop(1, n)
            def _(k):
                t, device = peer(hop(k, n))
                pltpu.make_async_remote_copy(
                    src_ref=part(src, t), dst_ref=place(dst, mine), send_sem=snd_sem.at[i],
                    recv_sem=rcv_sem.at[i], device_id=device, device_id_type=MESH,
                ).start()

            pltpu.make_async_copy(part(src, mine), place(dst, mine), loc_sem.at[i]).start()

        return start

    def finish(i, ring, src_all, dst_all, src, part, dst, place):
        n, mine, peer = rings[ring]
        pltpu.make_async_copy(part(src, mine), place(dst, mine), loc_sem.at[i]).wait()
        whole = pltpu.make_async_remote_copy(
            src_ref=src_all(src, n - 1), dst_ref=dst_all(dst, n - 1), send_sem=snd_sem.at[i],
            recv_sem=rcv_sem.at[i], device_id=peer(1)[1], device_id_type=MESH,
        )
        whole.wait_recv()
        return whole

    lead = lambda ref, t: ref.at[t]
    lead_n = lambda ref, n: ref.at[pl.ds(0, n)]
    second = lambda ref, t: ref.at[:, t]
    second_n = lambda ref, n: ref.at[:, pl.ds(0, n)]
    whole_ref = lambda ref, t: ref

    def exchange(i, ring, src, dst, part=lead, place=lead):
        src_all = second_n if part is second else lead_n
        dst_all = second_n if place is second else lead_n
        if part is whole_ref:
            src_all = lambda ref, n: dst_all(dst, n)
        start = stage(i, ring, src, part, dst, place)
        wait = lambda: finish(i, ring, src_all, dst_all, src, part, dst, place)
        return start, wait

    rows_a1 = exchange(0, "y", ra1, ra1r)
    rows_a2 = exchange(1, "u", ra2, ra2r)
    rows_b1 = exchange(2, "u", rb1, rb1r)
    rows_b2 = exchange(3, "y", rb2, rb2r)
    rowsx = exchange(4, "x", row, rowx, part=whole_ref)
    grad_a = (exchange(5, "y", ga0, ga0r), exchange(6, "u", ga1, ga1r), exchange(7, "u", ha0, ha0r), exchange(8, "y", ha1, ha1r))
    grad_b = (exchange(9, "y", gb0, gb0r), exchange(10, "u", gb1, gb1r), exchange(11, "u", hb0, hb0r), exchange(12, "y", hb1, hb1r))
    cross_a = exchange(13, "x", wa, xa)
    cross_b = exchange(14, "x", wb, xb)
    back_a1 = exchange(15, "u", ta1, ta1r)
    back_a2 = exchange(16, "y", ta2, ta2r)
    back_b1 = exchange(17, "y", tb1, tb1r)
    back_b2 = exchange(18, "u", tb2, tb2r)
    sent = []

    z = u // 2
    core = lax.rem(u, 2)

    def remote(i, src, dst, device):
        return pltpu.make_async_remote_copy(
            src_ref=src, dst_ref=dst, send_sem=snd_sem.at[i], recv_sem=rcv_sem.at[i],
            device_id=device, device_id_type=MESH,
        )

    def to_core(i, which, part, place):
        def start():
            @pl.loop(1, NU // 2)
            def _(k):
                t = lax.rem(z + hop(k, NU // 2), NU // 2)
                remote(i, part(t), place(u), (y * NU + t * 2 + which, mp)).start()

            @pl.when(core == which)
            def _():
                pltpu.make_async_copy(part(z), place(u), loc_sem.at[i]).start()

            @pl.when(core != which)
            def _():
                remote(i, part(z), place(u), (y * NU + z * 2 + which, mp)).start()

        def wait(gap):
            @pl.when(core == which)
            def _():
                pltpu.make_async_copy(part(z), place(u), loc_sem.at[i]).wait()
                remote(i, gap(NU - 1), gap(NU - 1), peer_u(1)[1]).wait_recv()

        def wait_send(gap):
            @pl.when(core == which)
            def _():
                remote(i, gap(NU // 2 - 1), gap(NU // 2 - 1), peer_u(1)[1]).wait_send()

            @pl.when(core != which)
            def _():
                remote(i, gap(NU // 2), gap(NU // 2), peer_u(1)[1]).wait_send()

        return start, wait, wait_send

    def along_y(i, part, place):
        def start():
            @pl.loop(1, NY)
            def _(k):
                t, device = peer_y(hop(k, NY))
                remote(i, part(t), place(y), device).start()

            pltpu.make_async_copy(part(y), place(y), loc_sem.at[i]).start()

        def wait(gap):
            pltpu.make_async_copy(part(y), place(y), loc_sem.at[i]).wait()
            remote(i, gap(NY - 1), gap(NY - 1), peer_y(1)[1]).wait_recv()

        def wait_send(gap):
            remote(i, gap(NY - 1), gap(NY - 1), peer_y(1)[1]).wait_send()

        return start, wait, wait_send

    def weight_path(i, out, d0, d1, got):
        first0 = to_core(i, 0, lambda t: out.at[:, t, 0], lambda s: d0.at[s])
        first1 = along_y(i + 1, lambda t: out.at[t, :, 1], lambda s: d1.at[s])
        then0 = along_y(i + 2, lambda t: d0.at[:, t], lambda s: got.at[s])
        then1 = to_core(i + 3, 1, lambda t: d1.at[:, t], lambda s: got.at[:, s])

        def first():
            first0[0]()
            first1[0]()

        def then():
            first0[1](lambda n: d0.at[pl.ds(0, n)])

            @pl.when(core == 0)
            def _():
                then0[0]()

            first1[1](lambda n: d1.at[pl.ds(0, n)])
            then1[0]()

        def last():
            @pl.when(core == 0)
            def _():
                then0[1](lambda n: got.at[pl.ds(0, n)])

            then1[1](lambda n: got.at[:, pl.ds(0, n)])

        def sends():
            first0[2](lambda n: d0.at[pl.ds(0, n)])
            first1[2](lambda n: d1.at[pl.ds(0, n)])

            @pl.when(core == 0)
            def _():
                then0[2](lambda n: got.at[pl.ds(0, n)])

            then1[2](lambda n: got.at[:, pl.ds(0, n)])

        return first, then, last, sends

    weight_a = weight_path(19, oa, da0, da1, wea)
    weight_b = weight_path(23, ob, db0, db1, web)

    p_a[...] = reorder(3, 4, 2)

    in_copies[9].wait()

    dest = jnp.broadcast_to(dest_ref[...], (128, 128))
    dest_t = dest.astype(F32).T.astype(I32)
    earlier = (dest == dest_t) & (iota((128, 128), 0) < iota((128, 128), 1))
    rank = jnp.sum(jnp.where(earlier, 1, 0), axis=0, keepdims=True)
    dest_row = dest_ref[...]
    live = iota((1, 128), 1) < counts_s[0]
    slot_y = jnp.where(live, dest_row * 2 + rank, -1)
    slot_u = jnp.where(live, (dest_row & 15) * 16 + (dest_row >> 4) * 2 + rank, -1)
    slots[...] = ones_where(iota((256, 128), 0) == jnp.broadcast_to(slot_y, (256, 128)))
    slots_u[...] = ones_where(iota((256, 128), 0) == jnp.broadcast_to(slot_u, (256, 128)))
    in_copies[1].wait()
    ra1[...] = mm(slots[...], rows[:, :256]).astype(BF).reshape(NY, 32, 256)
    rb1[...] = mm(slots_u[...], rows[:, 256:]).astype(BF).reshape(NU, 16, 256)

    pl.semaphore_wait(barrier, NY - 1 + NU - 1 + NX - 1)
    rows_a1[0]()
    rows_b1[0]()

    in_copies[0].wait()

    def partial(b):
        in_copies[5 + b].wait()
        return lax.dot_general(
            cot[...], hid[:, b * 256 : (b + 1) * 256], (((0,), (0,)), ((), ())), preferred_element_type=F32
        ).astype(BF)

    for b in range(2):
        lanes = slice(b * 128, (b + 1) * 128)
        part = partial(b)
        ga0[:, :, lanes] = part[:, :128].reshape(NY, 64, 128)
        gb0[:, :, lanes] = part[:, 128:].reshape(NY, 64, 128)
    grad_a[0][0]()
    for b in range(2):
        lanes = slice(b * 128, (b + 1) * 128)
        part = partial(2 + b)
        ha[:, lanes] = part[:, :128]
        hb[:, lanes] = part[:, 128:]
    ha0[...] = mm(p_a[...], ha[...]).astype(BF).reshape(NU, 32, 256)
    grad_a[2][0]()
    grad_b[0][0]()
    hb0[...] = mm(p_a[...], hb[...]).astype(BF).reshape(NU, 32, 256)
    grad_b[2][0]()

    p_at[...] = reorder(4, 3, 2)
    p_s[...] = reorder(3, 4, 1)
    p_st[...] = reorder(4, 3, 1)
    p_c[...] = reorder(2, 5, 2)
    p_ct[...] = reorder(5, 2, 2)
    in_copies[10].wait()
    old = jnp.broadcast_to(old_ref[...], (8, 128)).astype(F32).astype(BF)
    spread_b = ones_where(iota((128, 512), 0) == (iota((128, 512), 1) >> 2))
    col = iota((128, 512), 1)
    spread_a = ones_where(iota((128, 512), 0) == (((col >> 2) & 7) * NU + (col >> 5)))
    for spread, own in ((spread_a, own_a), (spread_b, own_b)):
        holder = mm(old, spread)[0:1].astype(I32)
        wanted = holder * 4 + (iota((1, 512), 1) & 3)
        own[...] = ones_where(iota((128, 512), 0) == jnp.broadcast_to(wanted, (128, 512)))

    sent.append(rows_a1[1]())
    ra2[...] = mm(p_s[...], ra1r[...].reshape(256, 256)).astype(BF).reshape(NU, 16, 256)
    sent.append(rows_b1[1]())
    rb2[...] = mm(p_st[...], rb1r[...].reshape(256, 256)).astype(BF).reshape(NY, 32, 256)

    def turn(grad, g0r, g1, h0r, h1):
        sent.append(grad[0][1]())
        g1[...] = mm(p_a[...], g0r[...].reshape(512, 256)).astype(BF).reshape(NU, 32, 256)
        grad[1][0]()
        sent.append(grad[2][1]())
        h1[...] = mm(p_at[...], h0r[...].reshape(512, 256)).astype(BF).reshape(NY, 64, 256)
        grad[3][0]()

    turn(grad_a, ga0r, ga1, ha0r, ha1)
    turn(grad_b, gb0r, gb1, hb0r, hb1)
    rows_a2[0]()
    rows_b2[0]()

    for i in (2, 3, 4):
        in_copies[i].wait()

    def step(grad, g1r, h1r, half, out, cross):
        for pair, own, recv, got in ((0, own_a, g1r, grad[1][1]), (2, own_b, h1r, grad[3][1])):
            sent.append(got())
            gradient = mm(own[...], recv[...].reshape(512, 256))
            for b in range(2):
                at = pl.ds(2 * (pair + b) + half, 128, stride=8)
                updated, first_new, second_new = adam_update(
                    gradient[:, b * 128 : (b + 1) * 128], mas[at, :], one[at, :], two[at, :]
                )
                mas_n[at, :] = updated
                one_n[at, :] = first_new
                two_n[at, :] = second_new
                out[pair + b] = updated.astype(BF)
        cross()

    def place_weights(got, x, table, out, start):
        sent.append(got())
        table[...] = mm(p_c[...], x[...].reshape(512, 128)).astype(BF).reshape(EXPERTS, 16, 128)

        @pl.loop(0, NY)
        def _(a):
            for b in range(NU):
                out[a, b // 2, b % 2] = table[new_s[a * NU + b]]

        start()

    step(grad_a, ga1r, ha1r, 0, wa, cross_a[0])
    place_weights(cross_a[1], xa, ya, oa, weight_a[0])
    step(grad_b, gb1r, hb1r, 1, wb, cross_b[0])
    place_weights(cross_b[1], xb, yb, ob, weight_b[0])

    sent.append(rows_a2[1]())
    row[:, :, :256] = ra2r[...]
    sent.append(rows_b2[1]())
    row[:, :, 256:] = mm(p_s[...], rb2r[...].reshape(256, 256)).astype(BF).reshape(NU, 16, 256)
    rowsx[0]()
    weight_a[1]()
    weight_b[1]()
    sent.append(rowsx[1]())
    for b in range(4):
        lanes = jnp.concatenate(
            [rowx[m, :, :, b * 128 : (b + 1) * 128].reshape(256, 128) for m in range(NX)], axis=1
        )
        turned = mm(lanes, p_ct[...]).astype(BF)
        rowp[:, b * 512 : (b + 1) * 512] = turned
        rowq[:, b * 512 : (b + 1) * 512] = mm(p_st[...], turned).astype(BF)

    weight_a[2]()
    out_a = mm(rowp[...], wea[...].reshape(2048, 128)).astype(BF)
    ta1[...] = out_a.reshape(NU, 16, 128)
    back_a1[0]()
    weight_b[2]()
    out_b = mm(rowq[...], web[...].reshape(2048, 128)).astype(BF)
    tb1[...] = out_b.reshape(NY, 32, 128)
    back_b1[0]()
    sent.append(back_a1[1]())
    ta2[...] = mm(p_st[...], ta1r[...].reshape(256, 128)).astype(BF).reshape(NY, 32, 128)
    back_a2[0]()
    sent.append(back_b1[1]())
    tb2[...] = mm(p_s[...], tb1r[...].reshape(256, 128)).astype(BF).reshape(NU, 16, 128)
    back_b2[0]()

    def pick(s, got):
        return lax.dot_general(
            s[...], got[...].reshape(256, 128), (((0,), (0,)), ((), ())), preferred_element_type=F32
        ).astype(BF)

    sent.append(back_a2[1]())
    proj[:, :128] = pick(slots, ta2r)
    sent.append(back_b2[1]())
    proj[:, 128:] = pick(slots_u, tb2r)
    for copy in sent:
        copy.wait_send()
    weight_a[3]()
    weight_b[3]()


def commit(a, b, c, d, a_o, b_o, c_o, d_o, sem):
    moves = ((a, a_o), (b, b_o), (c, c_o), (d, d_o))
    puts = [pltpu.make_async_copy(v, o, sem.at[i]) for i, (v, o) in enumerate(moves)]
    for put in puts:
        put.start()
    for put in puts:
        put.wait()


def body(
    grad_cot, grad_hidden, old_place, master, moment_one, moment_two, new_place, rows, dest, counts
):
    state = jax.ShapeDtypeStruct((1024, 128), F32)
    hbm = pl.BlockSpec(memory_space=pltpu.HBM)
    vmem = pl.BlockSpec(memory_space=pltpu.VMEM)
    smem = pl.BlockSpec(memory_space=pltpu.SMEM)
    pin = lambda x: pltpu.with_memory_space_constraint(x, pltpu.HBM)
    v = lambda *s: pltpu.VMEM(s, BF)
    f = lambda *s: pltpu.VMEM(s, F32)
    scratch = [
        v(1024, 512), v(1024, 1024), v(128, 512),
        f(1024, 128), f(1024, 128), f(1024, 128), pltpu.VMEM((1, 128), I32), pltpu.VMEM((1, 128), I32),
        v(512, 512), v(512, 512), v(512, 512), v(512, 512), v(256, 256), v(256, 256),
        v(128, 512), v(128, 512), v(256, 128), v(256, 128),
        v(8, 32, 256), v(8, 32, 256), v(16, 16, 256), v(16, 16, 256),
        v(16, 16, 256), v(16, 16, 256), v(8, 32, 256), v(8, 32, 256),
        v(16, 16, 512), v(4, 16, 16, 512), v(256, 2048), v(256, 2048),
        v(8, 64, 256), v(8, 64, 256), v(16, 32, 256), v(16, 32, 256),
        v(512, 256), v(16, 32, 256), v(16, 32, 256), v(8, 64, 256), v(8, 64, 256),
        v(8, 64, 256), v(8, 64, 256), v(16, 32, 256), v(16, 32, 256),
        v(512, 256), v(16, 32, 256), v(16, 32, 256), v(8, 64, 256), v(8, 64, 256),
        v(4, 128, 128), v(4, 128, 128), v(4, 128, 128), v(4, 128, 128), v(32, 16, 128), v(32, 16, 128),
        v(8, 8, 2, 16, 128), v(8, 8, 2, 16, 128),
        v(16, 8, 16, 128), v(8, 8, 16, 128), v(16, 8, 16, 128), v(8, 8, 16, 128),
        v(8, 16, 16, 128), v(8, 16, 16, 128),
        v(16, 16, 128), v(8, 32, 128), v(16, 16, 128), v(8, 32, 128),
        v(8, 32, 128), v(16, 16, 128), v(8, 32, 128), v(16, 16, 128),
        pltpu.SemaphoreType.DMA((11,)), pltpu.SemaphoreType.DMA((27,)),
        pltpu.SemaphoreType.DMA((27,)), pltpu.SemaphoreType.DMA((27,)),
    ]
    shapes = (state, state, state, jax.ShapeDtypeStruct((128, 256), BF))
    results = pl.pallas_call(
        kernel,
        out_shape=shapes,
        in_specs=[hbm, hbm, hbm, hbm, hbm, hbm, smem, hbm, hbm, smem],
        out_specs=(vmem,) * 4,
        scratch_shapes=scratch,
        compiler_params=pltpu.CompilerParams(
            collective_id=0, has_side_effects=True, vmem_limit_bytes=50331648
        ),
        name="whole_step",
    )(
        pin(grad_cot), pin(grad_hidden), pin(old_place.reshape(1, 128)), pin(master.reshape(1024, 128)),
        pin(moment_one.reshape(1024, 128)), pin(moment_two.reshape(1024, 128)), pin(new_place), pin(rows),
        pin(dest.reshape(1, 128)), counts,
    )
    updated, first_new, second_new, projected = pl.pallas_call(
        commit,
        out_shape=shapes,
        in_specs=[vmem] * 4,
        out_specs=(hbm,) * 4,
        scratch_shapes=[pltpu.SemaphoreType.DMA((4,))],
        compiler_params=pltpu.CompilerParams(vmem_limit_bytes=1048576),
        name="commit",
    )(*results)
    back = lambda a: a.reshape(EXPERTS, 1, 4096)
    return (back(updated), back(first_new), back(second_new), projected)


def solution(mesh):
    return jax.shard_map(
        body,
        mesh=mesh,
        in_specs=(
            P("dp", "mp"),
            P("dp", None),
            P(),
            P(None, "mp", "dp"),
            P(None, "mp", "dp"),
            P(None, "mp", "dp"),
            P(),
            P("dp", "mp"),
            P("dp"),
            P("dp"),
        ),
        out_specs=(P(None, "mp", "dp"), P(None, "mp", "dp"), P(None, "mp", "dp"), P("dp", "mp")),
        check_vma=False,
    )
```

```python
import jax
import jax.numpy as jnp
from jax import lax
from jax.experimental import pallas as pl
from jax.experimental.pallas import tpu as pltpu
from jax.sharding import PartitionSpec as P

MESH = pl.DeviceIdType.MESH
BF = jnp.bfloat16
F32 = jnp.float32
I32 = jnp.int32

NY = 8
NU = 16
NX = 4
EXPERTS = 32

beta_first = 0.9
beta_second = 0.95
learn_rate = 0.01
decay_rate = 0.1
adam_eps = 1e-08
bias_first = 1.0 - 0.9**10
bias_second = 1.0 - 0.95**10


def adam_update(gradient, master, moment_one, moment_two):
    first_new = beta_first * moment_one + (1.0 - beta_first) * gradient
    second_new = beta_second * moment_two + (1.0 - beta_second) * gradient * gradient
    step_dir = first_new / bias_first / (jnp.sqrt(second_new / bias_second) + adam_eps)
    updated = master - learn_rate * (step_dir + decay_rate * master)
    return (updated, first_new, second_new)


def mm(a, b):
    return jnp.dot(a, b, preferred_element_type=F32)


def ones_where(cond):
    return jnp.where(cond, 1.0, 0.0).astype(BF)


def iota(shape, dim):
    return lax.broadcasted_iota(I32, shape, dim)


def swap_index(r, inner_bits, outer_bits, low_bits):
    low = r & ((1 << low_bits) - 1)
    outer = (r >> low_bits) & ((1 << outer_bits) - 1)
    inner = r >> (low_bits + outer_bits)
    return (((outer << inner_bits) | inner) << low_bits) | low


def reorder(first_bits, second_bits, low_bits):
    n = 1 << (first_bits + second_bits + low_bits)
    source = swap_index(iota((n, n), 0), second_bits, first_bits, low_bits)
    return ones_where(iota((n, n), 1) == source)


def kernel(
    cot_h, hid_h, old_h, mas_h, one_h, two_h, new_s, rows_h, dest_h, counts_s,
    mas_n, one_n, two_n, proj,
    cot, hid, rows, mas, one, two, old_ref, dest_ref,
    p_a, p_at, p_c, p_ct, p_s, p_st, own_a, own_b, slots, slots_u,
    ra1, ra1r, ra2, ra2r, rb1, rb1r, rb2, rb2r, row, rowx, rowp, rowq,
    ga0, ga0r, ga1, ga1r, ha, ha0, ha0r, ha1, ha1r,
    gb0, gb0r, gb1, gb1r, hb, hb0, hb0r, hb1, hb1r,
    wa, wb, xa, xb, ya, yb, oa, ob, da0, da1, db0, db1, wea, web,
    ta1, tb1, ta1r, tb1r, ta2, tb2, ta2r, tb2r,
    in_sem, loc_sem, snd_sem, rcv_sem,
):
    me = lax.axis_index("dp")
    mp = lax.axis_index("mp")
    y = me // NU
    u = lax.rem(me, NU)

    def peer_y(k):
        t = lax.rem(y + k, NY)
        return t, (t * NU + u, mp)

    def peer_u(k):
        t = lax.rem(u + k, NU)
        return t, (y * NU + t, mp)

    def peer_x(k):
        t = lax.rem(mp + k, NX)
        return t, (me, t)

    def hop(k, n):
        return n // 2 + lax.rem(k + 1, 2) * (k // 2) - lax.rem(k, 2) * (k // 2)

    rings = {"y": (NY, y, peer_y), "u": (NU, u, peer_u), "x": (NX, mp, peer_x)}

    ins = [
        (cot_h, cot), (rows_h, rows), (mas_h, mas), (one_h, one), (two_h, two),
    ]
    for b in range(NX):
        at = pl.ds(b * 256, 256)
        ins.append((hid_h.at[:, at], hid.at[:, at]))
    ins += [(dest_h, dest_ref), (old_h, old_ref)]
    in_copies = [pltpu.make_async_copy(s, d, in_sem.at[i]) for i, (s, d) in enumerate(ins)]
    for i in (9, 1, 0, 5, 6, 7, 8, 10, 2, 3, 4):
        in_copies[i].start()

    barrier = pltpu.get_barrier_semaphore()
    for n, _, peer in rings.values():

        @pl.loop(1, n)
        def _(k):
            pl.semaphore_signal(barrier, inc=1, device_id=peer(k)[1], device_id_type=MESH)

    def stage(i, ring, src, part, dst, place):
        n, mine, peer = rings[ring]

        def start():
            @pl.loop(1, n)
            def _(k):
                t, device = peer(hop(k, n))
                pltpu.make_async_remote_copy(
                    src_ref=part(src, t), dst_ref=place(dst, mine), send_sem=snd_sem.at[i],
                    recv_sem=rcv_sem.at[i], device_id=device, device_id_type=MESH,
                ).start()

            pltpu.make_async_copy(part(src, mine), place(dst, mine), loc_sem.at[i]).start()

        return start

    def finish(i, ring, src_all, dst_all, src, part, dst, place):
        n, mine, peer = rings[ring]
        pltpu.make_async_copy(part(src, mine), place(dst, mine), loc_sem.at[i]).wait()
        whole = pltpu.make_async_remote_copy(
            src_ref=src_all(src, n - 1), dst_ref=dst_all(dst, n - 1), send_sem=snd_sem.at[i],
            recv_sem=rcv_sem.at[i], device_id=peer(1)[1], device_id_type=MESH,
        )
        whole.wait_recv()
        return whole

    lead = lambda ref, t: ref.at[t]
    lead_n = lambda ref, n: ref.at[pl.ds(0, n)]
    second = lambda ref, t: ref.at[:, t]
    second_n = lambda ref, n: ref.at[:, pl.ds(0, n)]
    whole_ref = lambda ref, t: ref

    def exchange(i, ring, src, dst, part=lead, place=lead):
        src_all = second_n if part is second else lead_n
        dst_all = second_n if place is second else lead_n
        if part is whole_ref:
            src_all = lambda ref, n: dst_all(dst, n)
        start = stage(i, ring, src, part, dst, place)
        wait = lambda: finish(i, ring, src_all, dst_all, src, part, dst, place)
        return start, wait

    rows_a1 = exchange(0, "y", ra1, ra1r)
    rows_a2 = exchange(1, "u", ra2, ra2r)
    rows_b1 = exchange(2, "u", rb1, rb1r)
    rows_b2 = exchange(3, "y", rb2, rb2r)
    rowsx = exchange(4, "x", row, rowx, part=whole_ref)
    grad_a = (exchange(5, "y", ga0, ga0r), exchange(6, "u", ga1, ga1r), exchange(7, "u", ha0, ha0r), exchange(8, "y", ha1, ha1r))
    grad_b = (exchange(9, "y", gb0, gb0r), exchange(10, "u", gb1, gb1r), exchange(11, "u", hb0, hb0r), exchange(12, "y", hb1, hb1r))
    cross_a = exchange(13, "x", wa, xa)
    cross_b = exchange(14, "x", wb, xb)
    back_a1 = exchange(15, "u", ta1, ta1r)
    back_a2 = exchange(16, "y", ta2, ta2r)
    back_b1 = exchange(17, "y", tb1, tb1r)
    back_b2 = exchange(18, "u", tb2, tb2r)
    sent = []

    z = u // 2
    core = lax.rem(u, 2)

    def remote(i, src, dst, device):
        return pltpu.make_async_remote_copy(
            src_ref=src, dst_ref=dst, send_sem=snd_sem.at[i], recv_sem=rcv_sem.at[i],
            device_id=device, device_id_type=MESH,
        )

    def to_core(i, which, part, place):
        def start():
            @pl.loop(1, NU // 2)
            def _(k):
                t = lax.rem(z + hop(k, NU // 2), NU // 2)
                remote(i, part(t), place(u), (y * NU + t * 2 + which, mp)).start()

            @pl.when(core == which)
            def _():
                pltpu.make_async_copy(part(z), place(u), loc_sem.at[i]).start()

            @pl.when(core != which)
            def _():
                remote(i, part(z), place(u), (y * NU + z * 2 + which, mp)).start()

        def wait(gap):
            @pl.when(core == which)
            def _():
                pltpu.make_async_copy(part(z), place(u), loc_sem.at[i]).wait()
                remote(i, gap(NU - 1), gap(NU - 1), peer_u(1)[1]).wait_recv()

        def wait_send(gap):
            @pl.when(core == which)
            def _():
                remote(i, gap(NU // 2 - 1), gap(NU // 2 - 1), peer_u(1)[1]).wait_send()

            @pl.when(core != which)
            def _():
                remote(i, gap(NU // 2), gap(NU // 2), peer_u(1)[1]).wait_send()

        return start, wait, wait_send

    def along_y(i, part, place):
        def start():
            @pl.loop(1, NY)
            def _(k):
                t, device = peer_y(hop(k, NY))
                remote(i, part(t), place(y), device).start()

            pltpu.make_async_copy(part(y), place(y), loc_sem.at[i]).start()

        def wait(gap):
            pltpu.make_async_copy(part(y), place(y), loc_sem.at[i]).wait()
            remote(i, gap(NY - 1), gap(NY - 1), peer_y(1)[1]).wait_recv()

        def wait_send(gap):
            remote(i, gap(NY - 1), gap(NY - 1), peer_y(1)[1]).wait_send()

        return start, wait, wait_send

    def weight_path(i, out, d0, d1, got):
        first0 = to_core(i, 0, lambda t: out.at[:, t, 0], lambda s: d0.at[s])
        first1 = along_y(i + 1, lambda t: out.at[t, :, 1], lambda s: d1.at[s])
        then0 = along_y(i + 2, lambda t: d0.at[:, t], lambda s: got.at[s])
        then1 = to_core(i + 3, 1, lambda t: d1.at[:, t], lambda s: got.at[:, s])

        def first():
            first0[0]()
            first1[0]()

        def then():
            first0[1](lambda n: d0.at[pl.ds(0, n)])

            @pl.when(core == 0)
            def _():
                then0[0]()

            first1[1](lambda n: d1.at[pl.ds(0, n)])
            then1[0]()

        def last():
            @pl.when(core == 0)
            def _():
                then0[1](lambda n: got.at[pl.ds(0, n)])

            then1[1](lambda n: got.at[:, pl.ds(0, n)])

        def sends():
            first0[2](lambda n: d0.at[pl.ds(0, n)])
            first1[2](lambda n: d1.at[pl.ds(0, n)])

            @pl.when(core == 0)
            def _():
                then0[2](lambda n: got.at[pl.ds(0, n)])

            then1[2](lambda n: got.at[:, pl.ds(0, n)])

        return first, then, last, sends

    weight_a = weight_path(19, oa, da0, da1, wea)
    weight_b = weight_path(23, ob, db0, db1, web)

    p_a[...] = reorder(3, 4, 2)

    in_copies[9].wait()

    dest = jnp.broadcast_to(dest_ref[...], (128, 128))
    dest_t = dest.astype(F32).T.astype(I32)
    earlier = (dest == dest_t) & (iota((128, 128), 0) < iota((128, 128), 1))
    rank = jnp.sum(jnp.where(earlier, 1, 0), axis=0, keepdims=True)
    dest_row = dest_ref[...]
    live = iota((1, 128), 1) < counts_s[0]
    slot_y = jnp.where(live, dest_row * 2 + rank, -1)
    slot_u = jnp.where(live, (dest_row & 15) * 16 + (dest_row >> 4) * 2 + rank, -1)
    slots[...] = ones_where(iota((256, 128), 0) == jnp.broadcast_to(slot_y, (256, 128)))
    slots_u[...] = ones_where(iota((256, 128), 0) == jnp.broadcast_to(slot_u, (256, 128)))
    in_copies[1].wait()
    ra1[...] = mm(slots[...], rows[:, :256]).astype(BF).reshape(NY, 32, 256)
    rb1[...] = mm(slots_u[...], rows[:, 256:]).astype(BF).reshape(NU, 16, 256)

    pl.semaphore_wait(barrier, NY - 1 + NU - 1 + NX - 1)
    rows_a1[0]()
    rows_b1[0]()

    in_copies[0].wait()

    def partial(b):
        in_copies[5 + b].wait()
        return lax.dot_general(
            cot[...], hid[:, b * 256 : (b + 1) * 256], (((0,), (0,)), ((), ())), preferred_element_type=F32
        ).astype(BF)

    for b in range(2):
        lanes = slice(b * 128, (b + 1) * 128)
        part = partial(b)
        ga0[:, :, lanes] = part[:, :128].reshape(NY, 64, 128)
        gb0[:, :, lanes] = part[:, 128:].reshape(NY, 64, 128)
    grad_a[0][0]()
    for b in range(2):
        lanes = slice(b * 128, (b + 1) * 128)
        part = partial(2 + b)
        ha[:, lanes] = part[:, :128]
        hb[:, lanes] = part[:, 128:]
    ha0[...] = mm(p_a[...], ha[...]).astype(BF).reshape(NU, 32, 256)
    grad_a[2][0]()
    grad_b[0][0]()
    hb0[...] = mm(p_a[...], hb[...]).astype(BF).reshape(NU, 32, 256)
    grad_b[2][0]()

    p_at[...] = reorder(4, 3, 2)
    p_s[...] = reorder(3, 4, 1)
    p_st[...] = reorder(4, 3, 1)
    p_c[...] = reorder(2, 5, 2)
    p_ct[...] = reorder(5, 2, 2)
    in_copies[10].wait()
    old = jnp.broadcast_to(old_ref[...], (8, 128)).astype(F32).astype(BF)
    spread_b = ones_where(iota((128, 512), 0) == (iota((128, 512), 1) >> 2))
    col = iota((128, 512), 1)
    spread_a = ones_where(iota((128, 512), 0) == (((col >> 2) & 7) * NU + (col >> 5)))
    for spread, own in ((spread_a, own_a), (spread_b, own_b)):
        holder = mm(old, spread)[0:1].astype(I32)
        wanted = holder * 4 + (iota((1, 512), 1) & 3)
        own[...] = ones_where(iota((128, 512), 0) == jnp.broadcast_to(wanted, (128, 512)))

    sent.append(rows_a1[1]())
    ra2[...] = mm(p_s[...], ra1r[...].reshape(256, 256)).astype(BF).reshape(NU, 16, 256)
    sent.append(rows_b1[1]())
    rb2[...] = mm(p_st[...], rb1r[...].reshape(256, 256)).astype(BF).reshape(NY, 32, 256)

    def turn(grad, g0r, g1, h0r, h1):
        sent.append(grad[0][1]())
        g1[...] = mm(p_a[...], g0r[...].reshape(512, 256)).astype(BF).reshape(NU, 32, 256)
        grad[1][0]()
        sent.append(grad[2][1]())
        h1[...] = mm(p_at[...], h0r[...].reshape(512, 256)).astype(BF).reshape(NY, 64, 256)
        grad[3][0]()

    turn(grad_a, ga0r, ga1, ha0r, ha1)
    turn(grad_b, gb0r, gb1, hb0r, hb1)
    rows_a2[0]()
    rows_b2[0]()

    for i in (2, 3, 4):
        in_copies[i].wait()

    def step(grad, g1r, h1r, half, out, cross):
        for pair, own, recv, got in ((0, own_a, g1r, grad[1][1]), (2, own_b, h1r, grad[3][1])):
            sent.append(got())
            gradient = mm(own[...], recv[...].reshape(512, 256))
            for b in range(2):
                at = pl.ds(2 * (pair + b) + half, 128, stride=8)
                updated, first_new, second_new = adam_update(
                    gradient[:, b * 128 : (b + 1) * 128], mas[at, :], one[at, :], two[at, :]
                )
                mas_n[at, :] = updated
                one_n[at, :] = first_new
                two_n[at, :] = second_new
                out[pair + b] = updated.astype(BF)
        cross()

    def place_weights(got, x, table, out, start):
        sent.append(got())
        table[...] = mm(p_c[...], x[...].reshape(512, 128)).astype(BF).reshape(EXPERTS, 16, 128)

        @pl.loop(0, NY)
        def _(a):
            for b in range(NU):
                out[a, b // 2, b % 2] = table[new_s[a * NU + b]]

        start()

    step(grad_a, ga1r, ha1r, 0, wa, cross_a[0])
    place_weights(cross_a[1], xa, ya, oa, weight_a[0])
    step(grad_b, gb1r, hb1r, 1, wb, cross_b[0])
    place_weights(cross_b[1], xb, yb, ob, weight_b[0])

    weight_a[1]()
    sent.append(rows_a2[1]())
    row[:, :, :256] = ra2r[...]
    sent.append(rows_b2[1]())
    row[:, :, 256:] = mm(p_s[...], rb2r[...].reshape(256, 256)).astype(BF).reshape(NU, 16, 256)
    rowsx[0]()
    weight_b[1]()
    sent.append(rowsx[1]())
    for b in range(4):
        lanes = jnp.concatenate(
            [rowx[m, :, :, b * 128 : (b + 1) * 128].reshape(256, 128) for m in range(NX)], axis=1
        )
        turned = mm(lanes, p_ct[...]).astype(BF)
        rowp[:, b * 512 : (b + 1) * 512] = turned
        rowq[:, b * 512 : (b + 1) * 512] = mm(p_st[...], turned).astype(BF)

    weight_a[2]()
    out_a = mm(rowp[...], wea[...].reshape(2048, 128)).astype(BF)
    ta1[...] = out_a.reshape(NU, 16, 128)
    back_a1[0]()
    weight_b[2]()
    out_b = mm(rowq[...], web[...].reshape(2048, 128)).astype(BF)
    tb1[...] = out_b.reshape(NY, 32, 128)
    back_b1[0]()
    sent.append(back_a1[1]())
    ta2[...] = mm(p_st[...], ta1r[...].reshape(256, 128)).astype(BF).reshape(NY, 32, 128)
    back_a2[0]()
    sent.append(back_b1[1]())
    tb2[...] = mm(p_s[...], tb1r[...].reshape(256, 128)).astype(BF).reshape(NU, 16, 128)
    back_b2[0]()

    def pick(s, got):
        return lax.dot_general(
            s[...], got[...].reshape(256, 128), (((0,), (0,)), ((), ())), preferred_element_type=F32
        ).astype(BF)

    sent.append(back_a2[1]())
    proj[:, :128] = pick(slots, ta2r)
    sent.append(back_b2[1]())
    proj[:, 128:] = pick(slots_u, tb2r)
    for copy in sent:
        copy.wait_send()
    weight_a[3]()
    weight_b[3]()


def commit(a, b, c, d, a_o, b_o, c_o, d_o, sem):
    moves = ((a, a_o), (b, b_o), (c, c_o), (d, d_o))
    puts = [pltpu.make_async_copy(v, o, sem.at[i]) for i, (v, o) in enumerate(moves)]
    for put in puts:
        put.start()
    for put in puts:
        put.wait()


def body(
    grad_cot, grad_hidden, old_place, master, moment_one, moment_two, new_place, rows, dest, counts
):
    state = jax.ShapeDtypeStruct((1024, 128), F32)
    hbm = pl.BlockSpec(memory_space=pltpu.HBM)
    vmem = pl.BlockSpec(memory_space=pltpu.VMEM)
    smem = pl.BlockSpec(memory_space=pltpu.SMEM)
    pin = lambda x: pltpu.with_memory_space_constraint(x, pltpu.HBM)
    v = lambda *s: pltpu.VMEM(s, BF)
    f = lambda *s: pltpu.VMEM(s, F32)
    scratch = [
        v(1024, 512), v(1024, 1024), v(128, 512),
        f(1024, 128), f(1024, 128), f(1024, 128), pltpu.VMEM((1, 128), I32), pltpu.VMEM((1, 128), I32),
        v(512, 512), v(512, 512), v(512, 512), v(512, 512), v(256, 256), v(256, 256),
        v(128, 512), v(128, 512), v(256, 128), v(256, 128),
        v(8, 32, 256), v(8, 32, 256), v(16, 16, 256), v(16, 16, 256),
        v(16, 16, 256), v(16, 16, 256), v(8, 32, 256), v(8, 32, 256),
        v(16, 16, 512), v(4, 16, 16, 512), v(256, 2048), v(256, 2048),
        v(8, 64, 256), v(8, 64, 256), v(16, 32, 256), v(16, 32, 256),
        v(512, 256), v(16, 32, 256), v(16, 32, 256), v(8, 64, 256), v(8, 64, 256),
        v(8, 64, 256), v(8, 64, 256), v(16, 32, 256), v(16, 32, 256),
        v(512, 256), v(16, 32, 256), v(16, 32, 256), v(8, 64, 256), v(8, 64, 256),
        v(4, 128, 128), v(4, 128, 128), v(4, 128, 128), v(4, 128, 128), v(32, 16, 128), v(32, 16, 128),
        v(8, 8, 2, 16, 128), v(8, 8, 2, 16, 128),
        v(16, 8, 16, 128), v(8, 8, 16, 128), v(16, 8, 16, 128), v(8, 8, 16, 128),
        v(8, 16, 16, 128), v(8, 16, 16, 128),
        v(16, 16, 128), v(8, 32, 128), v(16, 16, 128), v(8, 32, 128),
        v(8, 32, 128), v(16, 16, 128), v(8, 32, 128), v(16, 16, 128),
        pltpu.SemaphoreType.DMA((11,)), pltpu.SemaphoreType.DMA((27,)),
        pltpu.SemaphoreType.DMA((27,)), pltpu.SemaphoreType.DMA((27,)),
    ]
    shapes = (state, state, state, jax.ShapeDtypeStruct((128, 256), BF))
    results = pl.pallas_call(
        kernel,
        out_shape=shapes,
        in_specs=[hbm, hbm, hbm, hbm, hbm, hbm, smem, hbm, hbm, smem],
        out_specs=(vmem,) * 4,
        scratch_shapes=scratch,
        compiler_params=pltpu.CompilerParams(
            collective_id=0, has_side_effects=True, vmem_limit_bytes=50331648
        ),
        name="whole_step",
    )(
        pin(grad_cot), pin(grad_hidden), pin(old_place.reshape(1, 128)), pin(master.reshape(1024, 128)),
        pin(moment_one.reshape(1024, 128)), pin(moment_two.reshape(1024, 128)), pin(new_place), pin(rows),
        pin(dest.reshape(1, 128)), counts,
    )
    updated, first_new, second_new, projected = pl.pallas_call(
        commit,
        out_shape=shapes,
        in_specs=[vmem] * 4,
        out_specs=(hbm,) * 4,
        scratch_shapes=[pltpu.SemaphoreType.DMA((4,))],
        compiler_params=pltpu.CompilerParams(vmem_limit_bytes=1048576),
        name="commit",
    )(*results)
    back = lambda a: a.reshape(EXPERTS, 1, 4096)
    return (back(updated), back(first_new), back(second_new), projected)


def solution(mesh):
    return jax.shard_map(
        body,
        mesh=mesh,
        in_specs=(
            P("dp", "mp"),
            P("dp", None),
            P(),
            P(None, "mp", "dp"),
            P(None, "mp", "dp"),
            P(None, "mp", "dp"),
            P(),
            P("dp", "mp"),
            P("dp"),
            P("dp"),
        ),
        out_specs=(P(None, "mp", "dp"), P(None, "mp", "dp"), P(None, "mp", "dp"), P("dp", "mp")),
        check_vma=False,
    )
```
